128 devices in a mesh: ep: 8 (over z, core), dp: 16 (over y, x).
Axes of the slice: x: 4, y: 4, z: 4, core: 2. Of those that a mesh axis runs over, the one named last changes fastest.
Arguments:
- tokens: bfloat16 [32768, 1024], P(('ep', 'dp')), may hold values from -6 to 6
- lengths: int32 [8, 2], P('ep'), may hold values from 1 to 3072, 4096 in all within a row
- adapter_ids: int32 [8, 2], replicated, may hold values from 0 to 63
- expert_ids: int32 [32768, 8], P(('ep', 'dp')), may hold values from 0 to 31, all different within a row; in each aligned block of 256 rows (0 to 255, 256 to 511, ...) at most 96 rows name the same one
- attn_gain: bfloat16 [1024], replicated, may hold values from 0.5 to 1.5
- w_qkv: bfloat16 [1024, 2048], replicated, may hold values from -3 to 3
- w_out: bfloat16 [1024, 1024], replicated, may hold values from -0.1875 to 0.1875
- moe_gain: bfloat16 [1024], replicated, may hold values from 0.5 to 1.5
- w_router: bfloat16 [1024, 32], replicated, may hold values from -12 to 12
- w_gate_up: bfloat16 [32, 1024, 1024], P('ep'), may hold values from -0.1875 to 0.1875
- w_down: bfloat16 [32, 512, 1024], P('ep'), may hold values from -0.25 to 0.25
- adapter_in: bfloat16 [64, 1024, 64], P('dp'), may hold values from -0.1875 to 0.1875
- adapter_out: bfloat16 [64, 16, 4096], P('dp'), may hold values from -0.75 to 0.75
- adapter_expert: bfloat16 [64, 48, 512], P('dp'), may hold values from -0.75 to 0.75
Outputs:
- layer_out: bfloat16 [32768, 1024], P(('ep', 'dp'))
The draws below stay inside these ranges and needn't reach their ends.
Inputs may be any that keep to these rules, and one draw needn't show every extreme that they name: `lengths`: each row sums to 4096. `expert_ids`: each row names 8 different experts; among the 256 rows of one device no expert is named more than 96 times.
All inputs are finite; a program needn't handle non-finite values.
Results may differ from the reference program's by a relative error of at most 0.02.
The reference program's roundings to bfloat16 on the way count: a program that leaves them out, or rounds other values in their place, can miss the bound.
Values may be sent and summed in bfloat16 or wider, within the bound.
A program may use at most 256 MiB of HBM per device.

```python
import math
import jax
import jax.numpy as jnp
import numpy as np
from jax import lax

D = 1024
HEADS = 16
KV_HEADS = 8
HEAD = 64
EXPERTS = 32
FF = 512
TOPK = 8
RANK = 16
ADAPTERS = 64
REQS = 2
TOK_DEV = 256
CAP = 96
GROUP = 4096
TOKENS = 32768
QKV = 2048
N_EP = 8


def draw_w_qkv(key, part):
    total_cols = HEADS * HEAD + 2 * KV_HEADS * HEAD
    base = jax.random.truncated_normal(jax.random.fold_in(key, 11), -6.0, 6.0, (D, total_cols), jnp.float32) * D ** (-0.5)
    return base.astype(jnp.bfloat16)


def draw_w_router(key, part):
    base = jax.random.truncated_normal(jax.random.fold_in(key, 21), -6.0, 6.0, (D, EXPERTS), jnp.float32) * D ** (-0.5)
    return base.astype(jnp.bfloat16)


def touch_ends(drawn, key, smallest, largest):
    extent = drawn.shape
    index_at = [jax.random.randint(jax.random.fold_in(key, axis), (), 0, extent[axis]) for axis in range(len(extent))]
    drawn = drawn.at[tuple(index_at)].set(smallest)
    longest = extent.index(max(extent))
    index_at[longest] = (index_at[longest] + 1) % extent[longest]
    return drawn.at[tuple(index_at)].set(largest)


def block_scale(rng, shape, shards, least, largest):
    factor_of = 1.0
    for dim, shards_of in shards:
        heights = jax.random.uniform(jax.random.fold_in(jax.random.fold_in(rng, 6), dim), (shards_of,), jnp.float32, least / len(shards), largest / len(shards))
        factor_of = factor_of * jnp.repeat(jnp.exp(heights), shape[dim] // shards_of).reshape((-1,) + (1,) * (len(shape) - 1 - dim))
    return factor_of


def length_profile(count, total, most, slope):
    loads = [(1 << 20) // math.isqrt(rank ** slope) + 1 for rank in range(2, count + 1)]
    surplus, given = total - most - (count - 1), [1] * (count - 1)
    while surplus > 0:
        free = [i for i in range(count - 1) if given[i] < most]
        mass, remaining = sum([loads[i] for i in free]), surplus
        for i in free:
            extra = min(most - given[i], max(1, remaining * loads[i] // mass), surplus)
            given[i] = given[i] + extra
            surplus = surplus - extra
    return np.array([most] + given)


def ragged(stream_key, count, total, most, lean):
    if count == 2:
        one = jax.random.randint(stream_key, (), max(1, total - most), min(most, total - 1) + 1)
        return jnp.stack([one, total - one])
    sizes = jnp.asarray(length_profile(count, total, most, lean), jnp.int32)
    pairs = (count - 1) // 2
    giver, receiver = sizes[1:1 + 2 * pairs:2], sizes[2:2 + 2 * pairs:2]
    margin = jnp.minimum(giver - 1, most - receiver)
    passed = jax.random.randint(jax.random.fold_in(stream_key, 1), (pairs,), 0, 1 << 20) % (margin + 1)
    sizes = sizes.at[1:1 + 2 * pairs:2].set(giver - passed).at[2:2 + 2 * pairs:2].set(receiver + passed)
    return sizes[jax.random.permutation(jax.random.fold_in(stream_key, 2), count)]


def routed_block(key, own, number, rows, number_of, top, bound, skew):
    ranking = jax.random.permutation(key, number_of)
    packed, usual = portions_of(number_of, rows * top, bound, skew, True), portions_of(number_of, rows * top, bound, skew, False)
    places = jnp.arange(number_of)

    def named(sizes, rotation):
        used = int((sizes > 0).sum())
        fixed = max(1, used // 4)
        moved = fixed + (places - fixed + rotation * (used - fixed)) % max(1, number_of - fixed)
        return jnp.zeros((number_of,), jnp.int32).at[ranking[jnp.where(places < fixed, places, moved)]].set(jnp.asarray(sizes, jnp.int32))

    sizes = jnp.where(number % 4 == 0, named(packed, number // 4), named(usual, number - number // 4 - 1))
    mixed = jax.random.permutation(jax.random.fold_in(own, 3), number_of)
    donor, receiver = mixed[0:number_of // 2 * 2:2], mixed[1:number_of // 2 * 2:2]
    margin = jnp.minimum(sizes[donor] - 1, bound - sizes[receiver]) // 2
    margin = jnp.where((donor == ranking[0]) | (receiver == ranking[0]) | (sizes[receiver] == 0), 0, jnp.maximum(margin, 0))
    moved = jax.random.randint(jax.random.fold_in(own, 4), (number_of // 2,), 0, 1 << 20) % (margin + 1)
    sizes = sizes.at[donor].add(-moved).at[receiver].add(moved)
    items = jnp.searchsorted(jnp.cumsum(sizes), jnp.arange(rows * top), side="right").astype(jnp.int32)
    table = items.reshape(top, rows).T
    table = table[jax.random.permutation(jax.random.fold_in(own, 1), rows)]
    rotation = jax.random.randint(jax.random.fold_in(own, 2), (rows, 1), 0, top)
    return jnp.take_along_axis(table, (jnp.arange(top)[None, :] + rotation) % top, axis=1)


def portions_of(number_of, total, bound, skew, full):
    loads = [(1 << 20) // math.isqrt(grade ** skew) + 1 for grade in range(1, number_of + 1)]
    largest = bound if full else min(bound, max(-(-total // number_of), total * loads[0] // sum(loads)))
    least = 1 if total - largest >= number_of - 1 else 0
    given, rest = [largest] + [least] * (number_of - 1), total - largest - least * (number_of - 1)
    while rest > 0:
        free = [i for i in range(1, number_of) if given[i] < largest] or [i for i in range(1, number_of) if given[i] < bound]
        mass, remaining = sum([loads[i] for i in free]), rest
        for i in free:
            more = min(bound - given[i], max(1, remaining * loads[i] // mass), rest)
            given[i] = given[i] + more
            rest = rest - more
    return np.array(given)


def gaussian(own_key, shape, deviation, reach, split=(), kind=jnp.bfloat16):
    loudness = block_scale(own_key, shape, split, -0.22, 0.18) if split else 1.0
    drawn = jax.random.normal(own_key, shape, jnp.float32) * deviation * loudness
    return jnp.minimum(jnp.maximum(drawn, -reach), reach).astype(kind)


def setup_inputs(seed: int = 0) -> dict:
    key_of = jax.random.split(jax.random.key(seed), 15)
    tokens = gaussian(key_of[0], (TOKENS, D), 1.0, 6.0, ((0, 128),))
    lengths = jax.vmap(lambda own: ragged(own, REQS, GROUP, 3 * GROUP // 4, 2))(jax.random.split(key_of[1], N_EP)).reshape((N_EP, REQS)).astype(jnp.int32)
    adapter_ids = touch_ends(jax.random.randint(key_of[2], (N_EP, REQS), 0, ADAPTERS), jax.random.fold_in(key_of[2], 1), 0, ADAPTERS - 1).astype(jnp.int32)
    expert_ids_keys = jax.random.split(jax.random.fold_in(key_of[3], 1), TOKENS // TOK_DEV)
    expert_ids_turns = jax.random.permutation(jax.random.fold_in(key_of[3], 3), TOKENS // TOK_DEV)
    expert_ids = jax.vmap(lambda own, number: routed_block(jax.random.fold_in(key_of[3], 2), own, number, TOK_DEV, EXPERTS, TOPK, CAP, 1))(expert_ids_keys, expert_ids_turns).reshape((TOKENS, TOPK))
    attn_gain = jnp.clip(1.0 + 0.1 * jax.random.normal(key_of[4], (D,), jnp.float32), 0.5, 1.5).astype(jnp.bfloat16)
    w_qkv = draw_w_qkv(jax.random.fold_in(key_of[14], 71), 0)
    w_out = gaussian(key_of[6], (D, D), D ** -0.5, 0.1875)
    moe_gain = jnp.clip(1.0 + 0.1 * jax.random.normal(key_of[7], (D,), jnp.float32), 0.5, 1.5).astype(jnp.bfloat16)
    w_router = draw_w_router(jax.random.fold_in(key_of[14], 71), 0)
    w_gate_up = gaussian(key_of[9], (EXPERTS, D, 2 * FF), D ** -0.5, 0.1875, ((0, 8),))
    w_down = gaussian(key_of[10], (EXPERTS, FF, D), FF ** -0.5, 0.25, ((0, 8),))
    adapter_in = gaussian(key_of[11], (ADAPTERS, D, 4 * RANK), D ** -0.5, 0.1875, ((0, 16),))
    adapter_out = gaussian(key_of[12], (ADAPTERS, RANK, QKV + 2 * D), (4 * RANK) ** -0.5, 0.75, ((0, 16),))
    adapter_expert = gaussian(key_of[13], (ADAPTERS, 3 * RANK, FF), (4 * RANK) ** -0.5, 0.75, ((0, 16),))
    return {"tokens": tokens, "lengths": lengths, "adapter_ids": adapter_ids, "expert_ids": expert_ids, "attn_gain": attn_gain, "w_qkv": w_qkv, "w_out": w_out, "moe_gain": moe_gain, "w_router": w_router, "w_gate_up": w_gate_up, "w_down": w_down, "adapter_in": adapter_in, "adapter_out": adapter_out, "adapter_expert": adapter_expert}


EPS = 1e-06
THETA = 10000.0
NEG_BIG = -1e+30

def rms_norm(values_in, gain_vec):
    floats = values_in.astype(jnp.float32)
    meansq = lax.optimization_barrier(jnp.mean(floats * floats, axis=-1, keepdims=True))
    return (floats * lax.rsqrt(meansq + EPS) * gain_vec.astype(jnp.float32)).astype(jnp.bfloat16)

def rotate(vectors, position):
    half_dim = vectors.shape[-1] // 2
    frequency = THETA ** (-jnp.arange(half_dim, dtype=jnp.float32) / half_dim)
    angles = position.astype(jnp.float32)[:, None] * frequency[None, :]
    cosine = jnp.cos(angles)[:, None, :]
    sine_val = jnp.sin(angles)[:, None, :]
    first_half = vectors[..., :half_dim]
    second_half = vectors[..., half_dim:]
    return jnp.concatenate([first_half * cosine - second_half * sine_val, second_half * cosine + first_half * sine_val], axis=-1)

def request_layout(lengths_row, first_pos, row_count):
    position = (first_pos + jnp.arange(row_count, dtype=jnp.int32)).astype(jnp.int32)
    req_ends = jnp.cumsum(lengths_row).astype(jnp.int32)
    starts = (req_ends - lengths_row).astype(jnp.int32)
    request = lax.optimization_barrier(jnp.sum((position[:, None] >= req_ends[None, :]).astype(jnp.int32), axis=1)).astype(jnp.int32)
    slot_hot = request[:, None] == jnp.arange(lengths_row.shape[0], dtype=jnp.int32)[None, :]
    req_start = lax.optimization_barrier(jnp.sum(jnp.where(slot_hot, starts[None, :], 0), axis=1)).astype(jnp.int32)
    return (position, req_start, slot_hot)

def adapter_down(inputs, a_all, adapter_hot):
    tables = a_all.shape[0]
    count_r = a_all.shape[2]
    a_cat = jnp.transpose(a_all, (1, 0, 2)).reshape(inputs.shape[1], -1)
    coeffs = jnp.dot(inputs, a_cat, preferred_element_type=jnp.float32).reshape(inputs.shape[0], tables, count_r)
    return lax.optimization_barrier(jnp.sum(jnp.where(adapter_hot[:, :, None], coeffs, 0.0), axis=1)).astype(jnp.bfloat16)

def adapter_up(coeffs, b_all, adapter_hot):
    spread = jnp.where(adapter_hot[:, :, None], coeffs[:, None, :], jnp.zeros((), coeffs.dtype)).reshape(coeffs.shape[0], -1)
    return jnp.dot(spread, b_all.reshape(-1, b_all.shape[2]), preferred_element_type=jnp.float32)

def group_attention(operands):
    queries, keys_rot, values_v, position, req_start = operands
    group_len = queries.shape[0]
    block_len = math.gcd(group_len, 512)
    n_blocks = group_len // block_len
    kv_heads = keys_rot.shape[1]
    group_ratio = queries.shape[1] // kv_heads
    head_dim = queries.shape[2]
    score_scale = 1.0 / math.sqrt(head_dim)
    keys_f = keys_rot.astype(jnp.float32)
    vals_f = values_v.astype(jnp.float32)

    def one_block(block_idx):
        begin_row = block_idx * block_len
        query_blk = lax.dynamic_slice_in_dim(queries, begin_row, block_len, 0).astype(jnp.float32)
        query_blk = query_blk.reshape(block_len, kv_heads, group_ratio, head_dim)
        pos_blk = lax.dynamic_slice_in_dim(position, begin_row, block_len, 0)
        start_blk = lax.dynamic_slice_in_dim(req_start, begin_row, block_len, 0)
        scores = jnp.einsum('tgrd,sgd->tgrs', query_blk, keys_f, precision=lax.Precision.HIGHEST) * score_scale
        allowed = (position[None, :] >= start_blk[:, None]) & (position[None, :] <= pos_blk[:, None])
        allowed = allowed[:, None, None, :]
        scores = jnp.where(allowed, scores, NEG_BIG)
        row_max = lax.optimization_barrier(jnp.max(scores, axis=-1, keepdims=True))
        weights = jnp.where(allowed, jnp.exp(scores - row_max), 0.0)
        weight_sum = lax.optimization_barrier(jnp.sum(weights, axis=-1))
        weights_low = weights.astype(jnp.bfloat16).astype(jnp.float32)
        mixed_vals = jnp.einsum('tgrs,sgd->tgrd', weights_low, vals_f, precision=lax.Precision.HIGHEST)
        return (mixed_vals / weight_sum[..., None]).reshape(block_len, -1)
    blocks = lax.map(one_block, jnp.arange(n_blocks, dtype=jnp.int32))
    return blocks.reshape(group_len, -1).astype(jnp.bfloat16)

def reference(tokens, lengths, adapter_ids, expert_ids, attn_gain, w_qkv, w_out, moe_gain, w_router, w_gate_up, w_down, adapter_in, adapter_out, adapter_expert):
    q_width = HEADS * HEAD
    kv_width = KV_HEADS * HEAD
    qkv_width = q_width + 2 * kv_width
    position, req_start, slot_hot = jax.vmap(lambda lengths_row: request_layout(lengths_row, 0, GROUP))(lengths)
    adapter_tok = lax.optimization_barrier(jnp.sum(jnp.where(slot_hot, adapter_ids[:, None, :], 0), axis=2)).astype(jnp.int32).reshape(-1)
    adapter_hot = adapter_tok[:, None] == jnp.arange(ADAPTERS, dtype=jnp.int32)[None, :]
    rel_pos = (position - req_start).reshape(-1)
    normed = rms_norm(tokens, attn_gain)
    z_qkv = adapter_down(normed, adapter_in[:, :, 0:RANK], adapter_hot)
    projected = jnp.dot(normed, w_qkv, preferred_element_type=jnp.float32)
    projected = projected + adapter_up(z_qkv, adapter_out[:, :, 0:qkv_width], adapter_hot)
    queries = rotate(projected[:, :q_width].reshape(TOKENS, HEADS, HEAD), rel_pos).astype(jnp.bfloat16)
    keys_rot = rotate(projected[:, q_width:q_width + kv_width].reshape(TOKENS, KV_HEADS, HEAD), rel_pos).astype(jnp.bfloat16)
    values_v = projected[:, q_width + kv_width:].astype(jnp.bfloat16).reshape(TOKENS, KV_HEADS, HEAD)
    attended = lax.map(group_attention, (queries.reshape(N_EP, GROUP, HEADS, HEAD), keys_rot.reshape(N_EP, GROUP, KV_HEADS, HEAD), values_v.reshape(N_EP, GROUP, KV_HEADS, HEAD), position, req_start))
    attended = attended.reshape(TOKENS, q_width)
    z_out = adapter_down(attended, adapter_in[:, :, RANK:2 * RANK], adapter_hot)
    residual = tokens.astype(jnp.float32) + jnp.dot(attended, w_out, preferred_element_type=jnp.float32)
    residual = residual + adapter_up(z_out, adapter_out[:, :, qkv_width:qkv_width + D], adapter_hot)
    residual = residual.astype(jnp.bfloat16)
    normed_two = rms_norm(residual, moe_gain)
    logits = jnp.dot(normed_two, w_router, preferred_element_type=jnp.float32)
    gate_weights = jax.nn.softmax(jnp.take_along_axis(logits, expert_ids, axis=1), axis=1)
    z_experts = adapter_down(normed_two, adapter_in[:, :, 2 * RANK:4 * RANK], adapter_hot)
    b_gate = adapter_expert[:, 0:RANK]
    b_up = adapter_expert[:, RANK:2 * RANK]
    blank_blk = jnp.zeros_like(b_gate)
    b_joint = jnp.concatenate([jnp.concatenate([b_gate, blank_blk], axis=2), jnp.concatenate([blank_blk, b_up], axis=2)], axis=1)
    joint_delta = adapter_up(z_experts, b_joint, adapter_hot)
    a_down_t = jnp.transpose(adapter_expert[:, 2 * RANK:3 * RANK], (0, 2, 1))
    flat_expert = expert_ids.reshape(-1)
    flat_token = (jnp.arange(TOKENS * TOPK, dtype=jnp.int32) // TOPK).astype(jnp.int32)
    flat_gate = gate_weights.reshape(-1)
    sort_order = jnp.argsort(flat_expert, stable=True).astype(jnp.int32)
    counts = lax.optimization_barrier(jnp.sum((flat_expert[:, None] == jnp.arange(EXPERTS, dtype=jnp.int32)[None, :]).astype(jnp.int32), axis=0)).astype(jnp.int32)
    offsets = (jnp.cumsum(counts) - counts).astype(jnp.int32)
    block_rows = 512
    order_pad = jnp.concatenate([sort_order, jnp.zeros((block_rows,), jnp.int32)])

    def expert_loop(expert_idx, carried):
        w_pair = lax.dynamic_index_in_dim(w_gate_up, expert_idx, 0, keepdims=False)
        w_back = lax.dynamic_index_in_dim(w_down, expert_idx, 0, keepdims=False)
        n_blocks = (counts[expert_idx] + block_rows - 1) // block_rows

        def block_step(block_idx, inner):
            out_acc, coeff_acc = inner
            first_row = offsets[expert_idx] + block_idx * block_rows
            picked = lax.dynamic_slice_in_dim(order_pad, first_row, block_rows)
            valid_row = block_idx * block_rows + jnp.arange(block_rows, dtype=jnp.int32) < counts[expert_idx]
            tok_rows = flat_token[picked]
            pre_act = jnp.dot(normed_two[tok_rows], w_pair, preferred_element_type=jnp.float32) + joint_delta[tok_rows]
            hidden = (jax.nn.silu(pre_act[:, :FF]) * pre_act[:, FF:]).astype(jnp.bfloat16)
            expert_out = jnp.dot(hidden, w_back, preferred_element_type=jnp.float32).astype(jnp.bfloat16)
            a_rows = a_down_t[adapter_tok[tok_rows]]
            down_coeff = jnp.einsum('rh,rhk->rk', hidden.astype(jnp.float32), a_rows.astype(jnp.float32), precision=lax.Precision.HIGHEST).astype(jnp.bfloat16)
            weight_row = jnp.where(valid_row, flat_gate[picked], 0.0)
            out_acc = out_acc.at[tok_rows].add(weight_row[:, None] * expert_out.astype(jnp.float32))
            coeff_acc = coeff_acc.at[tok_rows].add(weight_row[:, None] * down_coeff.astype(jnp.float32))
            return (out_acc, coeff_acc)
        return lax.fori_loop(0, n_blocks, block_step, carried)
    exp_per = EXPERTS // N_EP

    def owner_loop(owner_idx, totals):
        fresh = (jnp.zeros((TOKENS, D), jnp.float32), jnp.zeros((TOKENS, RANK), jnp.float32))
        part_out, part_coeff = lax.fori_loop(owner_idx * exp_per, (owner_idx + 1) * exp_per, expert_loop, fresh)
        part_out = lax.optimization_barrier(part_out.astype(jnp.bfloat16)).astype(jnp.float32)
        part_coeff = lax.optimization_barrier(part_coeff.astype(jnp.bfloat16)).astype(jnp.float32)
        return (totals[0] + part_out, totals[1] + part_coeff)
    start_acc = (jnp.zeros((TOKENS, D), jnp.float32), jnp.zeros((TOKENS, RANK), jnp.float32))
    out_acc, coeff_acc = lax.fori_loop(0, N_EP, owner_loop, start_acc)
    coeff_sum = coeff_acc.astype(jnp.bfloat16)
    down_delta = adapter_up(coeff_sum, adapter_out[:, :, qkv_width + D:qkv_width + 2 * D], adapter_hot)
    return (residual.astype(jnp.float32) + out_acc + down_delta).astype(jnp.bfloat16)
```

```python
import math

import jax
import jax.numpy as jnp
from jax import lax
from jax.experimental import pallas as pl
from jax.experimental.pallas import tpu as pltpu
from jax.sharding import PartitionSpec as P

HEADS = 16
KV_HEADS = 8
HEAD = 64
CAP = 96
TOK = 256
D = 1024
FF = 512
QKV = 2048
N_DP = 16
N_EP = 8
EXP_LOCAL = 4
PIECE = 160

EPS = 1e-06
THETA = 10000.0
NEG_BIG = -1e30

BF = jnp.bfloat16
F32 = jnp.float32
MESH = pl.DeviceIdType.MESH
NT = (((1,), (1,)), ((), ()))
TN = (((0,), (0,)), ((), ()))


def dot(a, b):
    return jnp.dot(a, b, preferred_element_type=F32)


def dot_nt(a, b):
    return lax.dot_general(a, b, NT, preferred_element_type=F32)


def dot_tn(a, b):
    return lax.dot_general(a, b, TN, preferred_element_type=F32)


def other(me, off, count):
    return lax.rem(me + off, count)


def barrier(axes):
    sem = pltpu.get_barrier_semaphore()
    total = 0
    for axis, count in axes:
        me = lax.axis_index(axis)
        for off in range(1, count):
            pl.semaphore_signal(
                sem, inc=1, device_id={axis: other(me, off, count)}, device_id_type=MESH
            )
        total += count - 1
    pl.semaphore_wait(sem, total)


def push(src, dst, send_sem, recv_sem, axis, peer):
    copy = pltpu.make_async_remote_copy(
        src_ref=src,
        dst_ref=dst,
        send_sem=send_sem,
        recv_sem=recv_sem,
        device_id={axis: peer},
        device_id_type=MESH,
    )
    copy.start()
    return copy


def norm_rows(floats, gain_row):
    meansq = jnp.mean(floats * floats, axis=-1, keepdims=True)
    return (floats * lax.rsqrt(meansq + EPS) * gain_row).astype(BF)


def first_request_rows(lengths_ref, first_pos):
    pos = first_pos + lax.broadcasted_iota(jnp.int32, (TOK, 1), 0)
    return pos < lengths_ref[0, 0]


def first_request_lanes(lengths_ref, first_pos):
    pos = first_pos + lax.broadcasted_iota(jnp.int32, (1, TOK), 1)
    return pos < lengths_ref[0, 0]


def masked_pair(z, use, in_first):
    lo = z[:, use * 16 : use * 16 + 16]
    hi = z[:, 64 + use * 16 : 64 + use * 16 + 16]
    return jnp.where(in_first, lo, 0.0).astype(BF), jnp.where(in_first, 0.0, hi).astype(BF)


def up_block(pair, adapters_ref, block):
    halves = []
    for half in range(2):
        row = 64 + 32 * half
        halves.append(
            dot(pair[0], adapters_ref[block, row : row + 16, :])
            + dot(pair[1], adapters_ref[block, row + 16 : row + 32, :])
        )
    return jnp.concatenate(halves, axis=1)


def project_kernel(
    lengths_ref, tok_ref, gain_ref, w_ref, contrib_ref, cos_ref, sin_ref,
    recv_ref, adapters_ref,
    gathered, normed_scr, send_scr, s1, r1, s2, r2, s3, r3,
):
    me = lax.axis_index("dp")
    barrier([("dp", N_DP)])
    first = []
    for off in range(1, N_DP):
        peer = other(me, off, N_DP)
        first.append(
            push(contrib_ref.at[peer], gathered.at[me], s1.at[off], r1.at[off], "dp", peer)
        )
    normed_scr[...] = norm_rows(tok_ref[...].astype(F32), gain_ref[...].astype(F32))
    total = contrib_ref[me].astype(F32)
    for copy in first:
        copy.wait()
    for off in range(1, N_DP):
        total = total + gathered[other(me, off, N_DP)].astype(F32)
    adapters_ref[me] = total.astype(BF)
    second = []
    for off in range(1, N_DP):
        peer = other(me, off, N_DP)
        second.append(
            push(adapters_ref.at[me], adapters_ref.at[me], s2.at[off], r2.at[off], "dp", peer)
        )
    for copy in second:
        copy.wait()
    in_first = first_request_rows(lengths_ref, me * TOK)
    normed = normed_scr[...]
    z = dot(normed, adapters_ref[:, 0:64, :].reshape(D, 128))
    pair = masked_pair(z, 0, in_first)
    cosine = cos_ref[...]
    sine = sin_ref[...]

    def rope(head_t, scale):
        a = head_t[0:32]
        b = head_t[32:64]
        return (
            ((a * cosine - b * sine) * scale).astype(BF),
            ((b * cosine + a * sine) * scale).astype(BF),
        )

    for block in range(8):
        cols = slice(block * 256, block * 256 + 256)
        p_t = (dot(normed, w_ref[:, cols]) + up_block(pair, adapters_ref, block)).T
        for sub in range(4):
            head_t = p_t[sub * 64 : sub * 64 + 64]
            if block < 4:
                head = block * 4 + sub
                a, b = rope(head_t, 0.125)
                send_scr[head, 0:32, :] = a
                send_scr[head, 32:64, :] = b
            elif block < 6:
                head = (block - 4) * 4 + sub
                a, b = rope(head_t, 1.0)
                for twin in range(2):
                    send_scr[2 * head + twin, 64:96, :] = a
                    send_scr[2 * head + twin, 96:128, :] = b
            else:
                head = (block - 6) * 4 + sub
                v = head_t.astype(BF)
                for twin in range(2):
                    send_scr[2 * head + twin, 128:192, :] = v
    third = []
    for off in range(1, N_DP):
        peer = other(me, off, N_DP)
        third.append(push(send_scr.at[peer], recv_ref.at[me], s3.at[off], r3.at[off], "dp", peer))
    recv_ref[me] = send_scr[me]
    for copy in third:
        copy.wait()


def attention_kernel(lengths_ref, qkv_ref, out_ref, k_scr):
    length = lengths_ref[0, 0]
    for block in range(N_DP):
        k_scr[block] = qkv_ref[block, 64:128, :].astype(F32).T.astype(BF)
    lanes = lax.broadcasted_iota(jnp.int32, (1, TOK), 1)
    subs = lax.broadcasted_iota(jnp.int32, (TOK, 1), 0)

    def query_block(qb, unused):
        q_t = qkv_ref[qb, 0:64, :]
        q_first = qb * TOK
        qpos = q_first + lanes
        start = jnp.where(qpos >= length, length, 0)
        lo = jnp.where(q_first >= length, length, 0) // TOK
        mid = jnp.where(q_first + TOK - 1 >= length, (length + TOK - 1) // TOK, 0)
        mid = jnp.minimum(mid, qb)

        def step(kb, state, masked):
            run_max, run_sum, acc = state
            scores = dot(k_scr[kb], q_t)
            if masked:
                kpos = kb * TOK + subs
                allowed = (kpos >= start) & (kpos <= qpos)
                scores = jnp.where(allowed, scores, NEG_BIG)
            new_max = jnp.maximum(run_max, jnp.max(scores, axis=0, keepdims=True))
            weights = jnp.exp(scores - new_max)
            if masked:
                weights = jnp.where(allowed, weights, 0.0)
            fade = jnp.exp(run_max - new_max)
            new_sum = run_sum * fade + jnp.sum(weights, axis=0, keepdims=True)
            new_acc = acc * fade + dot(qkv_ref[kb, 128:192, :], weights.astype(BF))
            return new_max, new_sum, new_acc

        state = (
            jnp.full((1, TOK), NEG_BIG, F32),
            jnp.zeros((1, TOK), F32),
            jnp.zeros((HEAD, TOK), F32),
        )
        state = lax.fori_loop(lo, mid, lambda kb, s: step(kb, s, True), state)
        state = lax.fori_loop(mid, qb, lambda kb, s: step(kb, s, False), state)
        run_max, run_sum, acc = step(qb, state, True)
        out_ref[qb] = (acc / run_sum).astype(BF)
        return unused

    lax.fori_loop(0, N_DP, query_block, 0)


def route_kernel(
    lengths_ref, att_ref, tok_ref, adapters_ref, w_ref, gain_ref, router_ref, ids_ref,
    res_ref, x_ref, z_ref, rw_ref, ea_ref,
    att_t, x_scr, z_scr, rw_scr, ea_scr, s1, r1, s2, r2,
):
    me = lax.axis_index("dp")
    ep = lax.axis_index("ep")
    barrier([("dp", N_DP), ("ep", N_EP)])
    first = []
    for off in range(1, N_DP):
        peer = other(me, off, N_DP)
        first.append(push(att_ref.at[peer], att_t.at[me], s1.at[off], r1.at[off], "dp", peer))
    att_t[me] = att_ref[me]
    for use in range(3):
        for cb in range(4):
            ea_scr[use * 32 : use * 32 + 32, cb * 128 : cb * 128 + 128] = adapters_ref[
                use * 4 + cb, 128:160, :
            ]
    in_first = first_request_rows(lengths_ref, me * TOK)
    lane_first = first_request_lanes(lengths_ref, me * TOK)
    a_all = adapters_ref[:, 0:64, :].reshape(D, 128)
    for copy in first:
        copy.wait()
    attended = att_t[...].reshape(D, TOK).astype(F32).T.astype(BF)
    pair = masked_pair(dot(attended, a_all), 1, in_first)
    delta = jnp.concatenate([up_block(pair, adapters_ref, 8 + b) for b in range(4)], axis=1)
    residual = (tok_ref[...].astype(F32) + dot(attended, w_ref[...]) + delta).astype(BF)
    res_ref[...] = residual
    normed = norm_rows(residual.astype(F32), gain_ref[...].astype(F32))
    x_scr[...] = normed
    logits = dot_nt(router_ref[...], normed)
    experts = lax.broadcasted_iota(jnp.int32, (32, TOK), 0)
    ids = ids_ref[...]
    chosen = experts == ids[0:1]
    for k in range(1, 8):
        chosen = chosen | (experts == ids[k : k + 1])
    top = jnp.max(jnp.where(chosen, logits, NEG_BIG), axis=0, keepdims=True)
    raised = jnp.where(chosen, jnp.exp(jnp.where(chosen, logits - top, 0.0)), 0.0)
    gates = raised / jnp.sum(raised, axis=0, keepdims=True)
    before = (
        lax.broadcasted_iota(jnp.int32, (TOK, TOK), 0)
        < lax.broadcasted_iota(jnp.int32, (TOK, TOK), 1)
    ).astype(F32).astype(BF)
    rank = jnp.where(chosen, dot(chosen.astype(F32).astype(BF), before), -1.0)
    for owner in range(N_EP):
        rw_scr[owner, 0:4, :] = rank[owner * 4 : owner * 4 + 4]
        rw_scr[owner, 4:8, :] = gates[owner * 4 : owner * 4 + 4]
    z_t = dot(normed, a_all).T
    for use in range(2):
        lo = z_t[32 + use * 16 : 48 + use * 16]
        hi = z_t[96 + use * 16 : 112 + use * 16]
        z_scr[use * 32 : use * 32 + 16, :] = jnp.where(lane_first, lo, 0.0).astype(BF)
        z_scr[use * 32 + 16 : use * 32 + 32, :] = jnp.where(lane_first, 0.0, hi).astype(BF)
    second = []
    for off in range(1, N_EP):
        peer = other(ep, off, N_EP)
        for a, (src, dst) in enumerate(
            [
                (x_scr, x_ref.at[ep]),
                (z_scr, z_ref.at[ep]),
                (rw_scr.at[peer], rw_ref.at[ep]),
                (ea_scr, ea_ref.at[ep]),
            ]
        ):
            second.append(push(src, dst, s2.at[a, off], r2.at[a, off], "ep", peer))
    x_ref[ep] = x_scr[...]
    z_ref[ep] = z_scr[...]
    rw_ref[ep] = rw_scr[ep]
    ea_ref[ep] = ea_scr[...]
    for copy in second:
        copy.wait()


def expert_kernel(
    x_ref, z_ref, rw_ref, ea_ref, w_up_ref, w_down_ref, part_ref, coeff_ref,
    rows_scr, hid_scr, acc, coeff_acc,
):
    e = pl.program_id(0)

    @pl.when(e == 0)
    def _():
        acc[...] = jnp.zeros_like(acc)
        coeff_acc[...] = jnp.zeros_like(coeff_acc)

    slots = lax.broadcasted_iota(jnp.int32, (CAP, TOK), 0).astype(F32)

    def picker(j):
        return rw_ref[j, pl.ds(e, 1), :] == slots

    def gather(j, unused):
        pick = picker(j).astype(F32).astype(BF)
        rows_scr[pl.ds(pl.multiple_of(j * CAP, CAP), CAP), :] = dot(pick, x_ref[j]).astype(BF)
        return unused

    lax.fori_loop(0, N_EP, gather, 0)
    group = 2 * CAP
    for g in range(N_EP // 2):
        rows = slice(g * group, g * group + group)
        pre_gate = dot(rows_scr[rows, :], w_up_ref[0, :, 0:FF])
        pre_up = dot(rows_scr[rows, :], w_up_ref[0, :, FF:])
        for sub in range(2):
            j = 2 * g + sub
            local = slice(sub * CAP, sub * CAP + CAP)
            hit = picker(j)
            pick = hit.astype(F32).astype(BF)
            zr = dot_nt(pick, z_ref[j]).astype(BF)
            gate = pre_gate[local] + dot(zr[:, 0:32], ea_ref[j, 0:32, :])
            up = pre_up[local] + dot(zr[:, 32:64], ea_ref[j, 32:64, :])
            hid_scr[j * CAP : j * CAP + CAP, :] = (jax.nn.silu(gate) * up).astype(BF)
        out = dot(hid_scr[rows, :], w_down_ref[0])
        for sub in range(2):
            j = 2 * g + sub
            local = slice(sub * CAP, sub * CAP + CAP)
            hit = picker(j)
            pick = hit.astype(F32).astype(BF)
            weight = jnp.sum(
                jnp.where(hit, rw_ref[j, pl.ds(e + 4, 1), :], 0.0), axis=1, keepdims=True
            )
            scaled = (out[local] * weight).astype(BF)
            coeff = dot_nt(hid_scr[j * CAP : j * CAP + CAP, :], ea_ref[j, 64:96, :])
            acc[j] += dot_tn(pick, scaled)
            coeff_acc[j] += dot_tn((coeff * weight).astype(BF), pick)

    @pl.when(e == EXP_LOCAL - 1)
    def _():
        part_ref[...] = acc[...].astype(BF)
        coeff_ref[...] = coeff_acc[...].astype(BF)


def combine_kernel(
    lengths_ref, part_ref, coeff_ref, res_ref, adapters_ref, out_ref,
    part_in, coeff_in, s1, r1,
):
    ep = lax.axis_index("ep")
    me = lax.axis_index("dp")
    barrier([("ep", N_EP)])
    copies = []
    for off in range(1, N_EP):
        peer = other(ep, off, N_EP)
        copies.append(push(part_ref.at[peer], part_in.at[ep], s1.at[0, off], r1.at[0, off], "ep", peer))
        copies.append(push(coeff_ref.at[peer], coeff_in.at[ep], s1.at[1, off], r1.at[1, off], "ep", peer))
    lane_first = first_request_lanes(lengths_ref, me * TOK)
    total = part_ref[ep].astype(F32)
    csum = coeff_ref[ep].astype(F32)
    for copy in copies:
        copy.wait()
    for off in range(1, N_EP):
        peer = other(ep, off, N_EP)
        total = total + part_in[peer].astype(F32)
        csum = csum + coeff_in[peer].astype(F32)
    low = jnp.where(lane_first, csum[0:16], 0.0).astype(BF)
    high = jnp.where(lane_first, 0.0, csum[16:32]).astype(BF)
    for block in range(4):
        for half in range(2):
            row = 64 + 32 * half
            delta = dot_tn(low, adapters_ref[12 + block, row : row + 16, :]) + dot_tn(
                high, adapters_ref[12 + block, row + 16 : row + 32, :]
            )
            cols = slice(block * 256 + half * 128, block * 256 + half * 128 + 128)
            out_ref[:, cols] = (
                res_ref[:, cols].astype(F32) + total[:, cols] + delta
            ).astype(BF)


def vmem():
    return pl.BlockSpec(memory_space=pltpu.VMEM)


def smem():
    return pl.BlockSpec(memory_space=pltpu.SMEM)


def params(collective):
    return pltpu.CompilerParams(collective_id=collective, has_side_effects=True)


def shape(dims, dtype=BF):
    return jax.ShapeDtypeStruct(dims, dtype)


def pick_adapter(bank, wanted, first):
    chosen = jnp.zeros_like(bank[0])
    for i in range(bank.shape[0]):
        chosen = jnp.where(wanted == first + i, bank[i], chosen)
    return chosen


def per_device(
    tokens, lengths, adapter_ids, expert_ids, attn_gain, w_qkv, w_out, moe_gain,
    w_router, w_gate_up, w_down, adapter_in, adapter_out, adapter_expert,
):
    group_idx = lax.axis_index("ep")
    row_idx = lax.axis_index("dp")
    group_ids = lax.dynamic_index_in_dim(adapter_ids, group_idx, 0, keepdims=False)
    first = row_idx * adapter_in.shape[0]
    a_cat = jnp.concatenate(
        [pick_adapter(adapter_in, group_ids[r], first) for r in range(2)], axis=1
    )
    b_cat = jnp.concatenate(
        [pick_adapter(adapter_out, group_ids[r], first) for r in range(2)], axis=0
    )
    e_cat = jnp.stack([pick_adapter(adapter_expert, group_ids[r], first) for r in range(2)])
    b_pieces = jnp.transpose(b_cat.reshape(32, 16, 2, 128), (1, 2, 0, 3)).reshape(16, 64, 128)
    e_pieces = jnp.transpose(e_cat.reshape(2, 3, 16, 4, 128), (1, 3, 0, 2, 4)).reshape(12, 32, 128)
    e_pieces = jnp.pad(e_pieces, ((0, 4), (0, 0), (0, 0)))
    contrib = jnp.concatenate([a_cat.reshape(16, 64, 128), b_pieces, e_pieces], axis=1)

    position = row_idx * TOK + jnp.arange(TOK, dtype=jnp.int32)
    rel_pos = position - jnp.where(position >= lengths[0, 0], lengths[0, 0], 0)
    half = HEAD // 2
    frequency = THETA ** (-jnp.arange(half, dtype=F32) / half)
    angles = rel_pos.astype(F32)[None, :] * frequency[:, None]
    cosine = jnp.cos(angles)
    sine = jnp.sin(angles)

    dma = pltpu.SemaphoreType.DMA
    qkv_in, adapters = pl.pallas_call(
        project_kernel,
        name="project",
        out_shape=(shape((N_DP, 192, TOK)), shape((N_DP, PIECE, 128))),
        in_specs=[smem()] + [vmem()] * 6,
        out_specs=(vmem(), vmem()),
        scratch_shapes=[
            pltpu.VMEM((N_DP, PIECE, 128), BF),
            pltpu.VMEM((TOK, D), BF),
            pltpu.VMEM((N_DP, 192, TOK), BF),
        ]
        + [dma((N_DP,))] * 6,
        compiler_params=params(0),
    )(lengths, tokens, attn_gain[None, :], w_qkv, contrib, cosine, sine)

    attended = pl.pallas_call(
        attention_kernel,
        name="attention",
        out_shape=shape((N_DP, HEAD, TOK)),
        in_specs=[smem(), vmem()],
        out_specs=vmem(),
        scratch_shapes=[pltpu.VMEM((N_DP, TOK, HEAD), BF)],
    )(lengths, qkv_in)

    residual, x_all, z_all, rw_all, ea_all = pl.pallas_call(
        route_kernel,
        name="route",
        out_shape=(
            shape((TOK, D)),
            shape((N_EP, TOK, D)),
            shape((N_EP, 64, TOK)),
            shape((N_EP, 8, TOK), F32),
            shape((N_EP, 96, FF)),
        ),
        in_specs=[smem()] + [vmem()] * 7,
        out_specs=(vmem(),) * 5,
        scratch_shapes=[
            pltpu.VMEM((N_DP, HEAD, TOK), BF),
            pltpu.VMEM((TOK, D), BF),
            pltpu.VMEM((64, TOK), BF),
            pltpu.VMEM((N_EP, 8, TOK), F32),
            pltpu.VMEM((96, FF), BF),
            dma((N_DP,)),
            dma((N_DP,)),
            dma((4, N_EP)),
            dma((4, N_EP)),
        ],
        compiler_params=params(1),
    )(
        lengths, attended, tokens, adapters, w_out, moe_gain[None, :],
        jnp.transpose(w_router), jnp.transpose(expert_ids),
    )

    def whole(dims):
        return pl.BlockSpec(dims, lambda e: (0,) * len(dims))

    parts, coeffs = pl.pallas_call(
        expert_kernel,
        name="experts",
        grid=(EXP_LOCAL,),
        out_shape=(shape((N_EP, TOK, D)), shape((N_EP, 32, TOK))),
        in_specs=[
            whole((N_EP, TOK, D)),
            whole((N_EP, 64, TOK)),
            whole((N_EP, 8, TOK)),
            whole((N_EP, 96, FF)),
            pl.BlockSpec((1, D, 2 * FF), lambda e: (e, 0, 0)),
            pl.BlockSpec((1, FF, D), lambda e: (e, 0, 0)),
        ],
        out_specs=(whole((N_EP, TOK, D)), whole((N_EP, 32, TOK))),
        scratch_shapes=[
            pltpu.VMEM((N_EP * CAP, D), BF),
            pltpu.VMEM((N_EP * CAP, FF), BF),
            pltpu.VMEM((N_EP, TOK, D), F32),
            pltpu.VMEM((N_EP, 32, TOK), F32),
        ],
    )(x_all, z_all, rw_all, ea_all, w_gate_up, w_down)

    return pl.pallas_call(
        combine_kernel,
        name="combine",
        out_shape=shape((TOK, D)),
        in_specs=[smem()] + [vmem()] * 4,
        out_specs=vmem(),
        scratch_shapes=[
            pltpu.VMEM((N_EP, TOK, D), BF),
            pltpu.VMEM((N_EP, 32, TOK), BF),
            dma((2, N_EP)),
            dma((2, N_EP)),
        ],
        compiler_params=params(2),
    )(lengths, parts, coeffs, residual, adapters)


def solution(mesh):
    return jax.shard_map(
        per_device,
        mesh=mesh,
        in_specs=(
            P(("ep", "dp"), None),
            P("ep", None),
            P(),
            P(("ep", "dp"), None),
            P(),
            P(),
            P(),
            P(),
            P(),
            P("ep", None, None),
            P("ep", None, None),
            P("dp", None, None),
            P("dp", None, None),
            P("dp", None, None),
        ),
        out_specs=P(("ep", "dp"), None),
        check_vma=False,
    )
```

```python
import math

import jax
import jax.numpy as jnp
from jax import lax
from jax.experimental import pallas as pl
from jax.experimental.pallas import tpu as pltpu
from jax.sharding import PartitionSpec as P

HEADS = 16
KV_HEADS = 8
HEAD = 64
CAP = 96
TOK = 256
D = 1024
FF = 512
QKV = 2048
N_DP = 16
N_EP = 8
EXP_LOCAL = 4
PIECE = 160

EPS = 1e-06
THETA = 10000.0
NEG_BIG = -1e30

BF = jnp.bfloat16
F32 = jnp.float32
MESH = pl.DeviceIdType.MESH
NT = (((1,), (1,)), ((), ()))
TN = (((0,), (0,)), ((), ()))


def dot(a, b):
    return jnp.dot(a, b, preferred_element_type=F32)


def dot_nt(a, b):
    return lax.dot_general(a, b, NT, preferred_element_type=F32)


def dot_tn(a, b):
    return lax.dot_general(a, b, TN, preferred_element_type=F32)


def other(me, off, count):
    return lax.rem(me + off, count)


def barrier(axes):
    sem = pltpu.get_barrier_semaphore()
    total = 0
    for axis, count in axes:
        me = lax.axis_index(axis)
        for off in range(1, count):
            pl.semaphore_signal(
                sem, inc=1, device_id={axis: other(me, off, count)}, device_id_type=MESH
            )
        total += count - 1
    pl.semaphore_wait(sem, total)


def push(src, dst, send_sem, recv_sem, axis, peer):
    copy = pltpu.make_async_remote_copy(
        src_ref=src,
        dst_ref=dst,
        send_sem=send_sem,
        recv_sem=recv_sem,
        device_id={axis: peer},
        device_id_type=MESH,
    )
    copy.start()
    return copy


def ring_ids(ep):
    z = lax.div(ep, 2)
    c = lax.rem(ep, 2)
    up = lax.rem(z + 1, 4) * 2 + c
    down = lax.rem(z + 3, 4) * 2 + c
    far = lax.rem(z + 2, 4) * 2 + c
    sib = z * 2 + 1 - c
    return up, down, far, sib


class RingGather:
    def __init__(self, ep, src, dst, send, recv):
        self.ep, self.src, self.dst, self.send, self.recv = ep, src, dst, send, recv
        self.ids = ring_ids(ep)
        self.half = src.shape[0] // 2
        self.copies = []

    def push(self, src, dst, peer):
        i = len(self.copies)
        self.copies.append(push(src, dst, self.send.at[i], self.recv.at[i], "ep", peer))

    def start(self):
        up, down, far, sib = self.ids
        for peer in (up, down, sib):
            self.push(self.src, self.dst.at[self.ep], peer)

    def forward(self):
        up, down, far, sib = self.ids
        low, high = pl.ds(0, self.half), pl.ds(self.half, self.half)
        self.copies[0].wait_recv()
        self.push(self.dst.at[down, low], self.dst.at[down, low], up)
        self.push(self.dst.at[down], self.dst.at[down], sib)
        self.copies[1].wait_recv()
        self.push(self.dst.at[up, high], self.dst.at[up, high], down)
        self.push(self.dst.at[up], self.dst.at[up], sib)

    def last(self):
        up, down, far, sib = self.ids
        low, high = pl.ds(0, self.half), pl.ds(self.half, self.half)
        self.copies[3].wait_recv()
        self.push(self.dst.at[far, low], self.dst.at[far, low], sib)
        self.copies[5].wait_recv()
        self.push(self.dst.at[far, high], self.dst.at[far, high], sib)

    def finish(self):
        for i, copy in enumerate(self.copies):
            if i not in (0, 1, 3, 5):
                copy.wait_recv()
            copy.wait_send()


def norm_rows(floats, gain_row):
    meansq = jnp.mean(floats * floats, axis=-1, keepdims=True)
    return (floats * lax.rsqrt(meansq + EPS) * gain_row).astype(BF)


def first_request_rows(lengths_ref, first_pos):
    pos = first_pos + lax.broadcasted_iota(jnp.int32, (TOK, 1), 0)
    return pos < lengths_ref[0, 0]


def first_request_lanes(lengths_ref, first_pos):
    pos = first_pos + lax.broadcasted_iota(jnp.int32, (1, TOK), 1)
    return pos < lengths_ref[0, 0]


def masked_pair(z, use, in_first):
    lo = z[:, use * 16 : use * 16 + 16]
    hi = z[:, 64 + use * 16 : 64 + use * 16 + 16]
    return jnp.where(in_first, lo, 0.0).astype(BF), jnp.where(in_first, 0.0, hi).astype(BF)


def up_block(pair, adapters_ref, block):
    halves = []
    for half in range(2):
        row = 64 + 32 * half
        halves.append(
            dot(pair[0], adapters_ref[block, row : row + 16, :])
            + dot(pair[1], adapters_ref[block, row + 16 : row + 32, :])
        )
    return jnp.concatenate(halves, axis=1)


def project_kernel(
    lengths_ref, tok_ref, gain_ref, w_ref, contrib_ref, cos_ref, sin_ref,
    recv_ref, adapters_ref,
    gathered, normed_scr, send_scr, s1, r1, s2, r2, s3, r3,
):
    me = lax.axis_index("dp")
    barrier([("dp", N_DP)])
    first = []
    for off in range(1, N_DP):
        peer = other(me, off, N_DP)
        first.append(
            push(contrib_ref.at[peer], gathered.at[me], s1.at[off], r1.at[off], "dp", peer)
        )
    normed_scr[...] = norm_rows(tok_ref[...].astype(F32), gain_ref[...].astype(F32))
    total = contrib_ref[me].astype(F32)
    for copy in first:
        copy.wait()
    for off in range(1, N_DP):
        total = total + gathered[other(me, off, N_DP)].astype(F32)
    adapters_ref[me] = total.astype(BF)
    second = []
    for off in range(1, N_DP):
        peer = other(me, off, N_DP)
        second.append(
            push(adapters_ref.at[me], adapters_ref.at[me], s2.at[off], r2.at[off], "dp", peer)
        )
    for copy in second:
        copy.wait()
    in_first = first_request_rows(lengths_ref, me * TOK)
    normed = normed_scr[...]
    z = dot(normed, adapters_ref[:, 0:64, :].reshape(D, 128))
    pair = masked_pair(z, 0, in_first)
    cosine = cos_ref[...]
    sine = sin_ref[...]

    def rope(head_t, scale):
        a = head_t[0:32]
        b = head_t[32:64]
        return (
            ((a * cosine - b * sine) * scale).astype(BF),
            ((b * cosine + a * sine) * scale).astype(BF),
        )

    for block in range(8):
        cols = slice(block * 256, block * 256 + 256)
        p_t = (dot(normed, w_ref[:, cols]) + up_block(pair, adapters_ref, block)).T
        for sub in range(4):
            head_t = p_t[sub * 64 : sub * 64 + 64]
            if block < 4:
                head = block * 4 + sub
                a, b = rope(head_t, 0.125)
                send_scr[head, 0:32, :] = a
                send_scr[head, 32:64, :] = b
            elif block < 6:
                head = (block - 4) * 4 + sub
                a, b = rope(head_t, 1.0)
                for twin in range(2):
                    send_scr[2 * head + twin, 64:96, :] = a
                    send_scr[2 * head + twin, 96:128, :] = b
            else:
                head = (block - 6) * 4 + sub
                v = head_t.astype(BF)
                for twin in range(2):
                    send_scr[2 * head + twin, 128:192, :] = v
    third = []
    for off in range(1, N_DP):
        peer = other(me, off, N_DP)
        third.append(push(send_scr.at[peer], recv_ref.at[me], s3.at[off], r3.at[off], "dp", peer))
    recv_ref[me] = send_scr[me]
    for copy in third:
        copy.wait()


def attention_kernel(lengths_ref, qkv_ref, out_ref, k_scr):
    length = lengths_ref[0, 0]
    for block in range(N_DP):
        k_scr[block] = qkv_ref[block, 64:128, :].astype(F32).T.astype(BF)
    lanes = lax.broadcasted_iota(jnp.int32, (1, TOK), 1)
    subs = lax.broadcasted_iota(jnp.int32, (TOK, 1), 0)

    def query_block(qb, unused):
        q_t = qkv_ref[qb, 0:64, :]
        q_first = qb * TOK
        qpos = q_first + lanes
        start = jnp.where(qpos >= length, length, 0)
        lo = jnp.where(q_first >= length, length, 0) // TOK
        mid = jnp.where(q_first + TOK - 1 >= length, (length + TOK - 1) // TOK, 0)
        mid = jnp.minimum(mid, qb)

        def step(kb, state, masked):
            run_max, run_sum, acc = state
            scores = dot(k_scr[kb], q_t)
            if masked:
                kpos = kb * TOK + subs
                allowed = (kpos >= start) & (kpos <= qpos)
                scores = jnp.where(allowed, scores, NEG_BIG)
            new_max = jnp.maximum(run_max, jnp.max(scores, axis=0, keepdims=True))
            weights = jnp.exp(scores - new_max)
            if masked:
                weights = jnp.where(allowed, weights, 0.0)
            fade = jnp.exp(run_max - new_max)
            new_sum = run_sum * fade + jnp.sum(weights, axis=0, keepdims=True)
            new_acc = acc * fade + dot(qkv_ref[kb, 128:192, :], weights.astype(BF))
            return new_max, new_sum, new_acc

        state = (
            jnp.full((1, TOK), NEG_BIG, F32),
            jnp.zeros((1, TOK), F32),
            jnp.zeros((HEAD, TOK), F32),
        )
        state = lax.fori_loop(lo, mid, lambda kb, s: step(kb, s, True), state)
        state = lax.fori_loop(mid, qb, lambda kb, s: step(kb, s, False), state)
        run_max, run_sum, acc = step(qb, state, True)
        out_ref[qb] = (acc / run_sum).astype(BF)
        return unused

    lax.fori_loop(0, N_DP, query_block, 0)


def route_kernel(
    lengths_ref, att_ref, tok_ref, adapters_ref, w_ref, gain_ref, router_ref, ids_ref,
    res_ref, x_ref, z_ref, rw_ref, ea_ref,
    att_t, x_scr, z_scr, rw_scr, ea_scr, s1, r1, s2, r2, s3, r3,
):
    me = lax.axis_index("dp")
    ep = lax.axis_index("ep")
    barrier([("dp", N_DP), ("ep", N_EP)])
    first = []
    for off in range(1, N_DP):
        peer = other(me, off, N_DP)
        first.append(push(att_ref.at[peer], att_t.at[me], s1.at[off], r1.at[off], "dp", peer))
    att_t[me] = att_ref[me]
    for use in range(3):
        for cb in range(4):
            ea_scr[use * 32 : use * 32 + 32, cb * 128 : cb * 128 + 128] = adapters_ref[
                use * 4 + cb, 128:160, :
            ]
    ea_ring = RingGather(ep, ea_scr, ea_ref, s2.at[2], r2.at[2])
    ea_ring.start()
    ea_ref[ep] = ea_scr[...]
    in_first = first_request_rows(lengths_ref, me * TOK)
    lane_first = first_request_lanes(lengths_ref, me * TOK)
    a_all = adapters_ref[:, 0:64, :].reshape(D, 128)
    for copy in first:
        copy.wait()
    attended = att_t[...].reshape(D, TOK).astype(F32).T.astype(BF)
    pair = masked_pair(dot(attended, a_all), 1, in_first)
    delta = jnp.concatenate([up_block(pair, adapters_ref, 8 + b) for b in range(4)], axis=1)
    residual = (tok_ref[...].astype(F32) + dot(attended, w_ref[...]) + delta).astype(BF)
    res_ref[...] = residual
    normed = norm_rows(residual.astype(F32), gain_ref[...].astype(F32))
    x_scr[...] = normed
    logits = dot_nt(router_ref[...], normed)
    experts = lax.broadcasted_iota(jnp.int32, (32, TOK), 0)
    ids = ids_ref[...]
    chosen = experts == ids[0:1]
    for k in range(1, 8):
        chosen = chosen | (experts == ids[k : k + 1])
    top = jnp.max(jnp.where(chosen, logits, NEG_BIG), axis=0, keepdims=True)
    raised = jnp.where(chosen, jnp.exp(jnp.where(chosen, logits - top, 0.0)), 0.0)
    gates = raised / jnp.sum(raised, axis=0, keepdims=True)
    before = (
        lax.broadcasted_iota(jnp.int32, (TOK, TOK), 0)
        < lax.broadcasted_iota(jnp.int32, (TOK, TOK), 1)
    ).astype(F32).astype(BF)
    rank = jnp.where(chosen, dot(chosen.astype(F32).astype(BF), before), -1.0)
    for owner in range(N_EP):
        rw_scr[owner, 0:4, :] = rank[owner * 4 : owner * 4 + 4]
        rw_scr[owner, 4:8, :] = gates[owner * 4 : owner * 4 + 4]
    z_t = dot(normed, a_all).T
    for use in range(2):
        lo = z_t[32 + use * 16 : 48 + use * 16]
        hi = z_t[96 + use * 16 : 112 + use * 16]
        z_scr[use * 32 : use * 32 + 16, :] = jnp.where(lane_first, lo, 0.0).astype(BF)
        z_scr[use * 32 + 16 : use * 32 + 32, :] = jnp.where(lane_first, 0.0, hi).astype(BF)
    x_ring = RingGather(ep, x_scr, x_ref, s2.at[0], r2.at[0])
    z_ring = RingGather(ep, z_scr, z_ref, s2.at[1], r2.at[1])
    x_ring.start()
    z_ring.start()
    ea_ring.forward()
    second = []
    for off in range(1, N_EP):
        peer = other(ep, off, N_EP)
        second.append(push(rw_scr.at[peer], rw_ref.at[ep], s3.at[off], r3.at[off], "ep", peer))
    x_ref[ep] = x_scr[...]
    z_ref[ep] = z_scr[...]
    rw_ref[ep] = rw_scr[ep]
    ea_ring.last()
    x_ring.forward()
    z_ring.forward()
    x_ring.last()
    z_ring.last()
    for ring in (x_ring, z_ring, ea_ring):
        ring.finish()
    for copy in second:
        copy.wait()


def expert_kernel(
    x_ref, z_ref, rw_ref, ea_ref, w_up_ref, w_down_ref, part_ref, coeff_ref,
    rows_scr, hid_scr, acc, coeff_acc,
):
    e = pl.program_id(0)

    @pl.when(e == 0)
    def _():
        acc[...] = jnp.zeros_like(acc)
        coeff_acc[...] = jnp.zeros_like(coeff_acc)

    slots = lax.broadcasted_iota(jnp.int32, (CAP, TOK), 0).astype(F32)

    def picker(j):
        return rw_ref[j, pl.ds(e, 1), :] == slots

    def gather(j, unused):
        pick = picker(j).astype(F32).astype(BF)
        rows_scr[pl.ds(pl.multiple_of(j * CAP, CAP), CAP), :] = dot(pick, x_ref[j]).astype(BF)
        return unused

    lax.fori_loop(0, N_EP, gather, 0)
    group = 2 * CAP
    for g in range(N_EP // 2):
        rows = slice(g * group, g * group + group)
        pre_gate = dot(rows_scr[rows, :], w_up_ref[0, :, 0:FF])
        pre_up = dot(rows_scr[rows, :], w_up_ref[0, :, FF:])
        for sub in range(2):
            j = 2 * g + sub
            local = slice(sub * CAP, sub * CAP + CAP)
            hit = picker(j)
            pick = hit.astype(F32).astype(BF)
            zr = dot_nt(pick, z_ref[j]).astype(BF)
            gate = pre_gate[local] + dot(zr[:, 0:32], ea_ref[j, 0:32, :])
            up = pre_up[local] + dot(zr[:, 32:64], ea_ref[j, 32:64, :])
            hid_scr[j * CAP : j * CAP + CAP, :] = (jax.nn.silu(gate) * up).astype(BF)
        out = dot(hid_scr[rows, :], w_down_ref[0])
        for sub in range(2):
            j = 2 * g + sub
            local = slice(sub * CAP, sub * CAP + CAP)
            hit = picker(j)
            pick = hit.astype(F32).astype(BF)
            weight = jnp.sum(
                jnp.where(hit, rw_ref[j, pl.ds(e + 4, 1), :], 0.0), axis=1, keepdims=True
            )
            scaled = (out[local] * weight).astype(BF)
            coeff = dot_nt(hid_scr[j * CAP : j * CAP + CAP, :], ea_ref[j, 64:96, :])
            acc[j] += dot_tn(pick, scaled)
            coeff_acc[j] += dot_tn((coeff * weight).astype(BF), pick)

    @pl.when(e == EXP_LOCAL - 1)
    def _():
        part_ref[...] = acc[...].astype(BF)
        coeff_ref[...] = coeff_acc[...].astype(BF)


def combine_kernel(
    lengths_ref, part_ref, coeff_ref, res_ref, adapters_ref, out_ref,
    sib_in, sums, far_in, near_in, coeff_in, s1, r1, s2, r2,
):
    ep = lax.axis_index("ep")
    me = lax.axis_index("dp")
    barrier([("ep", N_EP)])
    up, down, far, sib = ring_ids(ep)
    half = TOK // 2
    low, high = pl.ds(0, half), pl.ds(half, half)
    c = lax.rem(ep, 2)
    order = [far, up, down, ep]
    pairs = []
    for i, dest in enumerate(order):
        pairs.append(
            push(part_ref.at[dest + 1 - 2 * c], sib_in.at[i], s1.at[i], r1.at[i], "ep", sib)
        )
    copies = []
    for off in range(1, N_EP):
        peer = other(ep, off, N_EP)
        copies.append(push(coeff_ref.at[peer], coeff_in.at[ep], s2.at[off], r2.at[off], "ep", peer))

    def pair_sum(i):
        pairs[i].wait_recv()
        return part_ref[order[i]].astype(F32) + sib_in[i].astype(F32)

    sums[0] = pair_sum(0).astype(BF)
    hop = [
        push(sums.at[0, low], far_in.at[0], s1.at[4], r1.at[4], "ep", up),
        push(sums.at[0, high], far_in.at[1], s1.at[5], r1.at[5], "ep", down),
    ]
    up_sum = pair_sum(1)
    sums[1, half:, :] = up_sum[half:].astype(BF)
    hop.append(push(sums.at[1, high], near_in.at[0, high], s1.at[6], r1.at[6], "ep", up))
    down_sum = pair_sum(2)
    sums[2, 0:half, :] = down_sum[0:half].astype(BF)
    hop.append(push(sums.at[2, low], near_in.at[1, low], s1.at[7], r1.at[7], "ep", down))
    hop[0].wait_recv()
    sums[1, 0:half, :] = (up_sum[0:half] + far_in[0].astype(F32)).astype(BF)
    hop.append(push(sums.at[1, low], near_in.at[0, low], s1.at[8], r1.at[8], "ep", up))
    hop[1].wait_recv()
    sums[2, half:, :] = (down_sum[half:] + far_in[1].astype(F32)).astype(BF)
    hop.append(push(sums.at[2, high], near_in.at[1, high], s1.at[9], r1.at[9], "ep", down))
    lane_first = first_request_lanes(lengths_ref, me * TOK)
    total = pair_sum(3)
    csum = coeff_ref[ep].astype(F32)
    for copy in copies:
        copy.wait()
    for off in range(1, N_EP):
        csum = csum + coeff_in[other(ep, off, N_EP)].astype(F32)
    for copy in hop[2:]:
        copy.wait_recv()
    total = total + near_in[0].astype(F32) + near_in[1].astype(F32)
    for copy in pairs + hop:
        copy.wait_send()
    lo_rows = jnp.where(lane_first, csum[0:16], 0.0).astype(BF)
    hi_rows = jnp.where(lane_first, 0.0, csum[16:32]).astype(BF)
    for block in range(4):
        for half in range(2):
            row = 64 + 32 * half
            delta = dot_tn(lo_rows, adapters_ref[12 + block, row : row + 16, :]) + dot_tn(
                hi_rows, adapters_ref[12 + block, row + 16 : row + 32, :]
            )
            cols = slice(block * 256 + half * 128, block * 256 + half * 128 + 128)
            out_ref[:, cols] = (
                res_ref[:, cols].astype(F32) + total[:, cols] + delta
            ).astype(BF)


def vmem():
    return pl.BlockSpec(memory_space=pltpu.VMEM)


def smem():
    return pl.BlockSpec(memory_space=pltpu.SMEM)


def params(collective):
    return pltpu.CompilerParams(collective_id=collective, has_side_effects=True)


def shape(dims, dtype=BF):
    return jax.ShapeDtypeStruct(dims, dtype)


def pick_adapter(bank, wanted, first):
    chosen = jnp.zeros_like(bank[0])
    for i in range(bank.shape[0]):
        chosen = jnp.where(wanted == first + i, bank[i], chosen)
    return chosen


def per_device(
    tokens, lengths, adapter_ids, expert_ids, attn_gain, w_qkv, w_out, moe_gain,
    w_router, w_gate_up, w_down, adapter_in, adapter_out, adapter_expert,
):
    group_idx = lax.axis_index("ep")
    row_idx = lax.axis_index("dp")
    group_ids = lax.dynamic_index_in_dim(adapter_ids, group_idx, 0, keepdims=False)
    first = row_idx * adapter_in.shape[0]
    a_cat = jnp.concatenate(
        [pick_adapter(adapter_in, group_ids[r], first) for r in range(2)], axis=1
    )
    b_cat = jnp.concatenate(
        [pick_adapter(adapter_out, group_ids[r], first) for r in range(2)], axis=0
    )
    e_cat = jnp.stack([pick_adapter(adapter_expert, group_ids[r], first) for r in range(2)])
    b_pieces = jnp.transpose(b_cat.reshape(32, 16, 2, 128), (1, 2, 0, 3)).reshape(16, 64, 128)
    e_pieces = jnp.transpose(e_cat.reshape(2, 3, 16, 4, 128), (1, 3, 0, 2, 4)).reshape(12, 32, 128)
    e_pieces = jnp.pad(e_pieces, ((0, 4), (0, 0), (0, 0)))
    contrib = jnp.concatenate([a_cat.reshape(16, 64, 128), b_pieces, e_pieces], axis=1)

    position = row_idx * TOK + jnp.arange(TOK, dtype=jnp.int32)
    rel_pos = position - jnp.where(position >= lengths[0, 0], lengths[0, 0], 0)
    half = HEAD // 2
    frequency = THETA ** (-jnp.arange(half, dtype=F32) / half)
    angles = rel_pos.astype(F32)[None, :] * frequency[:, None]
    cosine = jnp.cos(angles)
    sine = jnp.sin(angles)

    dma = pltpu.SemaphoreType.DMA
    qkv_in, adapters = pl.pallas_call(
        project_kernel,
        name="project",
        out_shape=(shape((N_DP, 192, TOK)), shape((N_DP, PIECE, 128))),
        in_specs=[smem()] + [vmem()] * 6,
        out_specs=(vmem(), vmem()),
        scratch_shapes=[
            pltpu.VMEM((N_DP, PIECE, 128), BF),
            pltpu.VMEM((TOK, D), BF),
            pltpu.VMEM((N_DP, 192, TOK), BF),
        ]
        + [dma((N_DP,))] * 6,
        compiler_params=params(0),
    )(lengths, tokens, attn_gain[None, :], w_qkv, contrib, cosine, sine)

    attended = pl.pallas_call(
        attention_kernel,
        name="attention",
        out_shape=shape((N_DP, HEAD, TOK)),
        in_specs=[smem(), vmem()],
        out_specs=vmem(),
        scratch_shapes=[pltpu.VMEM((N_DP, TOK, HEAD), BF)],
    )(lengths, qkv_in)

    residual, x_all, z_all, rw_all, ea_all = pl.pallas_call(
        route_kernel,
        name="route",
        out_shape=(
            shape((TOK, D)),
            shape((N_EP, TOK, D)),
            shape((N_EP, 64, TOK)),
            shape((N_EP, 8, TOK), F32),
            shape((N_EP, 96, FF)),
        ),
        in_specs=[smem()] + [vmem()] * 7,
        out_specs=(vmem(),) * 5,
        scratch_shapes=[
            pltpu.VMEM((N_DP, HEAD, TOK), BF),
            pltpu.VMEM((TOK, D), BF),
            pltpu.VMEM((64, TOK), BF),
            pltpu.VMEM((N_EP, 8, TOK), F32),
            pltpu.VMEM((96, FF), BF),
            dma((N_DP,)),
            dma((N_DP,)),
            dma((3, 9)),
            dma((3, 9)),
            dma((N_EP,)),
            dma((N_EP,)),
        ],
        compiler_params=params(1),
    )(
        lengths, attended, tokens, adapters, w_out, moe_gain[None, :],
        jnp.transpose(w_router), jnp.transpose(expert_ids),
    )

    def whole(dims):
        return pl.BlockSpec(dims, lambda e: (0,) * len(dims))

    parts, coeffs = pl.pallas_call(
        expert_kernel,
        name="experts",
        grid=(EXP_LOCAL,),
        out_shape=(shape((N_EP, TOK, D)), shape((N_EP, 32, TOK))),
        in_specs=[
            whole((N_EP, TOK, D)),
            whole((N_EP, 64, TOK)),
            whole((N_EP, 8, TOK)),
            whole((N_EP, 96, FF)),
            pl.BlockSpec((1, D, 2 * FF), lambda e: (e, 0, 0)),
            pl.BlockSpec((1, FF, D), lambda e: (e, 0, 0)),
        ],
        out_specs=(whole((N_EP, TOK, D)), whole((N_EP, 32, TOK))),
        scratch_shapes=[
            pltpu.VMEM((N_EP * CAP, D), BF),
            pltpu.VMEM((N_EP * CAP, FF), BF),
            pltpu.VMEM((N_EP, TOK, D), F32),
            pltpu.VMEM((N_EP, 32, TOK), F32),
        ],
    )(x_all, z_all, rw_all, ea_all, w_gate_up, w_down)

    return pl.pallas_call(
        combine_kernel,
        name="combine",
        out_shape=shape((TOK, D)),
        in_specs=[smem()] + [vmem()] * 4,
        out_specs=vmem(),
        scratch_shapes=[
            pltpu.VMEM((4, TOK, D), BF),
            pltpu.VMEM((3, TOK, D), BF),
            pltpu.VMEM((2, TOK // 2, D), BF),
            pltpu.VMEM((2, TOK, D), BF),
            pltpu.VMEM((N_EP, 32, TOK), BF),
            dma((10,)),
            dma((10,)),
            dma((N_EP,)),
            dma((N_EP,)),
        ],
        compiler_params=params(2),
    )(lengths, parts, coeffs, residual, adapters)


def solution(mesh):
    return jax.shard_map(
        per_device,
        mesh=mesh,
        in_specs=(
            P(("ep", "dp"), None),
            P("ep", None),
            P(),
            P(("ep", "dp"), None),
            P(),
            P(),
            P(),
            P(),
            P(),
            P("ep", None, None),
            P("ep", None, None),
            P("dp", None, None),
            P("dp", None, None),
            P("dp", None, None),
        ),
        out_specs=P(("ep", "dp"), None),
        check_vma=False,
    )
```

```python
import math

import jax
import jax.numpy as jnp
from jax import lax
from jax.experimental import pallas as pl
from jax.experimental.pallas import tpu as pltpu
from jax.sharding import PartitionSpec as P

HEADS = 16
KV_HEADS = 8
HEAD = 64
CAP = 96
TOK = 256
D = 1024
FF = 512
QKV = 2048
N_DP = 16
N_EP = 8
EXP_LOCAL = 4
AQ = 512
AK = 512

EPS = 1e-06
THETA = 10000.0
NEG_BIG = -1e30

BF = jnp.bfloat16
F32 = jnp.float32
MESH = pl.DeviceIdType.MESH
NT = (((1,), (1,)), ((), ()))
TN = (((0,), (0,)), ((), ()))


def dot(a, b):
    return jnp.dot(a, b, preferred_element_type=F32)


def dot_nt(a, b):
    return lax.dot_general(a, b, NT, preferred_element_type=F32)


def dot_tn(a, b):
    return lax.dot_general(a, b, TN, preferred_element_type=F32)


def other(me, off, count):
    return lax.rem(me + off, count)


def greet(axes):
    sem = pltpu.get_barrier_semaphore()
    total = 0
    for axis, count in axes:
        me = lax.axis_index(axis)
        for off in range(1, count):
            pl.semaphore_signal(
                sem, inc=1, device_id={axis: other(me, off, count)}, device_id_type=MESH
            )
        total += count - 1
    return sem, total


def barrier(axes):
    sem, total = greet(axes)
    pl.semaphore_wait(sem, total)


def push(src, dst, send_sem, recv_sem, axis, peer):
    copy = pltpu.make_async_remote_copy(
        src_ref=src,
        dst_ref=dst,
        send_sem=send_sem,
        recv_sem=recv_sem,
        device_id={axis: peer},
        device_id_type=MESH,
    )
    copy.start()
    return copy


def ring_ids(ep):
    z = lax.div(ep, 2)
    c = lax.rem(ep, 2)
    up = lax.rem(z + 1, 4) * 2 + c
    down = lax.rem(z + 3, 4) * 2 + c
    far = lax.rem(z + 2, 4) * 2 + c
    sib = z * 2 + 1 - c
    return up, down, far, sib


class RingGather:
    def __init__(self, ep, src, dst, send, recv):
        self.ep, self.src, self.dst, self.send, self.recv = ep, src, dst, send, recv
        self.ids = ring_ids(ep)
        self.half = src.shape[0] // 2
        self.copies = []

    def push(self, src, dst, peer):
        i = len(self.copies)
        self.copies.append(push(src, dst, self.send.at[i], self.recv.at[i], "ep", peer))

    def start(self):
        up, down, far, sib = self.ids
        for peer in (up, down, sib):
            self.push(self.src, self.dst.at[self.ep], peer)

    def forward(self):
        up, down, far, sib = self.ids
        low, high = pl.ds(0, self.half), pl.ds(self.half, self.half)
        self.copies[0].wait_recv()
        self.push(self.dst.at[down, low], self.dst.at[down, low], up)
        self.push(self.dst.at[down], self.dst.at[down], sib)
        self.copies[1].wait_recv()
        self.push(self.dst.at[up, high], self.dst.at[up, high], down)
        self.push(self.dst.at[up], self.dst.at[up], sib)

    def last(self):
        up, down, far, sib = self.ids
        low, high = pl.ds(0, self.half), pl.ds(self.half, self.half)
        self.copies[3].wait_recv()
        self.push(self.dst.at[far, low], self.dst.at[far, low], sib)
        self.copies[5].wait_recv()
        self.push(self.dst.at[far, high], self.dst.at[far, high], sib)

    def finish(self):
        for i, copy in enumerate(self.copies):
            if i not in (0, 1, 3, 5):
                copy.wait_recv()
            copy.wait_send()


def norm_rows(floats, gain_row):
    meansq = jnp.mean(floats * floats, axis=-1, keepdims=True)
    return (floats * lax.rsqrt(meansq + EPS) * gain_row).astype(BF)


def first_request_rows(lengths_ref, first_pos):
    pos = first_pos + lax.broadcasted_iota(jnp.int32, (TOK, 1), 0)
    return pos < lengths_ref[0, 0]


def first_request_lanes(lengths_ref, first_pos):
    pos = first_pos + lax.broadcasted_iota(jnp.int32, (1, TOK), 1)
    return pos < lengths_ref[0, 0]


def masked_pair(z, use, in_first):
    lo = z[:, use * 16 : use * 16 + 16]
    hi = z[:, 64 + use * 16 : 64 + use * 16 + 16]
    return jnp.where(in_first, lo, 0.0).astype(BF), jnp.where(in_first, 0.0, hi).astype(BF)


def up_block(pair, pieces_ref, block, row):
    return dot(pair[0], pieces_ref[block, row : row + 16, :]) + dot(
        pair[1], pieces_ref[block, row + 16 : row + 32, :]
    )


def exchange(src, dst, send_sem, recv_sem, me, rows=None):
    copies = []
    for off in range(1, N_DP):
        peer = other(me, off, N_DP)
        from_ref, to_ref = src.at[peer], dst.at[me]
        if rows is not None:
            from_ref, to_ref = src.at[peer, rows], dst.at[me, rows]
        copies.append(push(from_ref, to_ref, send_sem.at[off], recv_sem.at[off], "dp", peer))
    return copies


def sum_pieces(own_ref, gathered, me):
    total = own_ref[me].astype(F32)
    for off in range(1, N_DP):
        total = total + gathered[other(me, off, N_DP)].astype(F32)
    return total.astype(BF)


def share(ref, send_sem, recv_sem, me):
    copies = []
    for off in range(1, N_DP):
        peer = other(me, off, N_DP)
        copies.append(push(ref.at[me], ref.at[me], send_sem.at[off], recv_sem.at[off], "dp", peer))
    return copies


def project_kernel(
    lengths_ref, ids_ref, tok_ref, gain_ref, w_ref, in_bank, out_bank, exp_bank, freq_ref,
    recv_ref, main_ref, rest_ref,
    main_own, rest_own, main_in, rest_in, normed_scr, base_scr, send_scr,
    s1, r1, s2, r2, s3, r3, s4, r4, s5, r5, s6, r6,
):
    me = lax.axis_index("dp")
    ep = lax.axis_index("ep")
    greeted, expected = greet([("dp", N_DP)])
    for p in range(12, N_DP):
        rest_own[p, 32:64, :] = jnp.zeros((32, 128), BF)
    halves = []
    for r in range(2):
        local = ids_ref[ep, r] - me * 4
        held = (local >= 0) & (local < 4)
        at = jnp.clip(local, 0, 3)
        halves.append(jnp.where(held, in_bank[at].astype(F32), 0.0))
        out_rows = jnp.where(held, out_bank[at].astype(F32), 0.0).astype(BF)
        exp_rows = jnp.where(held, exp_bank[at].astype(F32), 0.0).astype(BF)
        rows = slice(16 * r, 16 * r + 16)
        for p in range(N_DP):
            main_own[p, 64 + 16 * r : 80 + 16 * r, :] = out_rows[:, p * 128 : p * 128 + 128]
            rest_own[p, rows, :] = out_rows[:, QKV + p * 128 : QKV + p * 128 + 128]
        for use in range(3):
            for cb in range(4):
                rest_own[use * 4 + cb, 32 + 16 * r : 48 + 16 * r, :] = exp_rows[
                    use * 16 : use * 16 + 16, cb * 128 : cb * 128 + 128
                ]
    a_cat = jnp.concatenate(halves, axis=1).astype(BF)
    for p in range(N_DP):
        main_own[p, 0:64, :] = a_cat[p * 64 : p * 64 + 64]
    pl.semaphore_wait(greeted, expected)
    main_1 = exchange(main_own, main_in, s1, r1, me)
    rest_1 = exchange(rest_own, rest_in, s2, r2, me)
    normed = norm_rows(tok_ref[...].astype(F32), gain_ref[...].astype(F32)[None, :])
    normed_scr[...] = normed
    base_scr[:, D:] = dot(normed, w_ref[:, D:])
    pos = me * TOK + lax.broadcasted_iota(jnp.int32, (1, TOK), 1)
    rel_pos = (pos - jnp.where(pos >= lengths_ref[0, 0], lengths_ref[0, 0], 0)).astype(F32)
    angles = freq_ref[...] * rel_pos
    cosine = jnp.cos(angles)
    sine = jnp.sin(angles)
    for copy in main_1:
        copy.wait()
    main_ref[me] = sum_pieces(main_own, main_in, me)
    main_2 = share(main_ref, s3, r3, me)
    base_scr[:, 0:D] = dot(normed_scr[...], w_ref[:, 0:D])
    for copy in rest_1:
        copy.wait()
    rest_ref[me] = sum_pieces(rest_own, rest_in, me)
    rest_2 = share(rest_ref, s4, r4, me)
    in_first = first_request_rows(lengths_ref, me * TOK)
    for copy in main_2:
        copy.wait()
    z = dot(normed_scr[...], main_ref[:, 0:64, :].reshape(D, 128))
    pair = masked_pair(z, 0, in_first)

    def rope(head_t, scale):
        a = head_t[0:32]
        b = head_t[32:64]
        return (
            ((a * cosine - b * sine) * scale).astype(BF),
            ((b * cosine + a * sine) * scale).astype(BF),
        )

    def heads_of(block):
        cols = slice(block * 128, block * 128 + 128)
        p_t = (base_scr[:, cols] + up_block(pair, main_ref, block, 64)).T
        return p_t[0:64], p_t[64:128]

    for block in range(8, 12):
        for sub, head_t in enumerate(heads_of(block)):
            head = (block - 8) * 2 + sub
            a, b = rope(head_t, 1.0)
            for twin in range(2):
                send_scr[2 * head + twin, 64:96, :] = a
                send_scr[2 * head + twin, 96:128, :] = b
    for block in range(12, 16):
        for sub, head_t in enumerate(heads_of(block)):
            head = (block - 12) * 2 + sub
            v = head_t.astype(BF)
            for twin in range(2):
                send_scr[2 * head + twin, 128:192, :] = v
    kv = exchange(send_scr, recv_ref, s5, r5, me, pl.ds(64, 128))
    for block in range(8):
        for sub, head_t in enumerate(heads_of(block)):
            head = block * 2 + sub
            a, b = rope(head_t, 0.125)
            send_scr[head, 0:32, :] = a
            send_scr[head, 32:64, :] = b
    q = exchange(send_scr, recv_ref, s6, r6, me, pl.ds(0, 64))
    recv_ref[me] = send_scr[me]
    for copy in rest_2 + kv + q:
        copy.wait()


def attention_kernel(lengths_ref, qkv_ref, out_ref, k_scr):
    length = lengths_ref[0, 0]
    for block in range(N_DP):
        rows = slice(block * TOK, block * TOK + TOK)
        k_scr[rows, :] = qkv_ref[block, 64:128, :].astype(F32).T.astype(BF)
    nq = AQ // TOK
    nk = AK // TOK
    lanes = lax.broadcasted_iota(jnp.int32, (1, AQ), 1)
    subs = lax.broadcasted_iota(jnp.int32, (AK, 1), 0)

    def query_block(qb, unused):
        q_t = jnp.concatenate([qkv_ref[qb * nq + i, 0:64, :] for i in range(nq)], axis=1)
        q_first = qb * AQ
        qpos = q_first + lanes
        start = jnp.where(qpos >= length, length, 0)
        lo = jnp.where(q_first >= length, length, 0) // AK
        mid = jnp.where(q_first + AQ - 1 >= length, (length + AK - 1) // AK, 0)
        mid = jnp.minimum(mid, qb)

        def step(kb, state, masked):
            run_max, run_sum, acc = state
            scores = dot(k_scr[pl.ds(pl.multiple_of(kb * AK, AK), AK), :], q_t)
            if masked:
                kpos = kb * AK + subs
                allowed = (kpos >= start) & (kpos <= qpos)
                scores = jnp.where(allowed, scores, NEG_BIG)
            new_max = jnp.maximum(run_max, jnp.max(scores, axis=0, keepdims=True))
            weights = jnp.exp(scores - new_max)
            if masked:
                weights = jnp.where(allowed, weights, 0.0)
            fade = jnp.exp(run_max - new_max)
            new_sum = run_sum * fade + jnp.sum(weights, axis=0, keepdims=True)
            low = weights.astype(BF)
            new_acc = acc * fade
            for i in range(nk):
                new_acc = new_acc + dot(
                    qkv_ref[kb * nk + i, 128:192, :], low[i * TOK : i * TOK + TOK]
                )
            return new_max, new_sum, new_acc

        state = (
            jnp.full((1, AQ), NEG_BIG, F32),
            jnp.zeros((1, AQ), F32),
            jnp.zeros((HEAD, AQ), F32),
        )
        state = lax.fori_loop(lo, mid, lambda kb, s: step(kb, s, True), state)
        state = lax.fori_loop(mid, qb, lambda kb, s: step(kb, s, False), state)
        run_max, run_sum, acc = step(qb, state, True)
        out = (acc / run_sum).astype(BF)
        for i in range(nq):
            out_ref[qb * nq + i] = out[:, i * TOK : i * TOK + TOK]
        return unused

    lax.fori_loop(0, N_DP // nq, query_block, 0)


def route_kernel(
    lengths_ref, att_ref, tok_ref, main_ref, rest_ref, w_ref, gain_ref, router_ref, ids_ref,
    res_ref, x_ref, z_ref, rw_ref, ea_ref,
    att_t, x_scr, z_scr, rw_scr, ea_scr, s1, r1, s2, r2, s3, r3,
):
    me = lax.axis_index("dp")
    ep = lax.axis_index("ep")
    barrier([("dp", N_DP), ("ep", N_EP)])
    first = []
    for off in range(1, N_DP):
        peer = other(me, off, N_DP)
        first.append(push(att_ref.at[peer], att_t.at[me], s1.at[off], r1.at[off], "dp", peer))
    att_t[me] = att_ref[me]
    for use in range(3):
        for cb in range(4):
            ea_scr[use * 32 : use * 32 + 32, cb * 128 : cb * 128 + 128] = rest_ref[
                use * 4 + cb, 32:64, :
            ]
    ea_ring = RingGather(ep, ea_scr, ea_ref, s2.at[2], r2.at[2])
    ea_ring.start()
    ea_ref[ep] = ea_scr[...]
    in_first = first_request_rows(lengths_ref, me * TOK)
    lane_first = first_request_lanes(lengths_ref, me * TOK)
    a_all = main_ref[:, 0:64, :].reshape(D, 128)
    for copy in first:
        copy.wait()
    attended = att_t[...].reshape(D, TOK).astype(F32).T.astype(BF)
    pair = masked_pair(dot(attended, a_all), 1, in_first)
    delta = jnp.concatenate([up_block(pair, rest_ref, b, 0) for b in range(8)], axis=1)
    residual = (tok_ref[...].astype(F32) + dot(attended, w_ref[...]) + delta).astype(BF)
    res_ref[...] = residual
    normed = norm_rows(residual.astype(F32), gain_ref[...].astype(F32)[None, :])
    x_scr[...] = normed
    logits = dot_nt(router_ref[...], normed)
    experts = lax.broadcasted_iota(jnp.int32, (32, TOK), 0)
    ids = ids_ref[...]
    chosen = experts == ids[0:1]
    for k in range(1, 8):
        chosen = chosen | (experts == ids[k : k + 1])
    top = jnp.max(jnp.where(chosen, logits, NEG_BIG), axis=0, keepdims=True)
    raised = jnp.where(chosen, jnp.exp(jnp.where(chosen, logits - top, 0.0)), 0.0)
    gates = raised / jnp.sum(raised, axis=0, keepdims=True)
    before = (
        lax.broadcasted_iota(jnp.int32, (TOK, TOK), 0)
        < lax.broadcasted_iota(jnp.int32, (TOK, TOK), 1)
    ).astype(F32).astype(BF)
    rank = jnp.where(chosen, dot(chosen.astype(F32).astype(BF), before), -1.0)
    for owner in range(N_EP):
        rw_scr[owner, 0:4, :] = rank[owner * 4 : owner * 4 + 4]
        rw_scr[owner, 4:8, :] = gates[owner * 4 : owner * 4 + 4]
    z_t = dot(normed, a_all).T
    for use in range(2):
        lo = z_t[32 + use * 16 : 48 + use * 16]
        hi = z_t[96 + use * 16 : 112 + use * 16]
        z_scr[use * 32 : use * 32 + 16, :] = jnp.where(lane_first, lo, 0.0).astype(BF)
        z_scr[use * 32 + 16 : use * 32 + 32, :] = jnp.where(lane_first, 0.0, hi).astype(BF)
    x_ring = RingGather(ep, x_scr, x_ref, s2.at[0], r2.at[0])
    z_ring = RingGather(ep, z_scr, z_ref, s2.at[1], r2.at[1])
    x_ring.start()
    z_ring.start()
    ea_ring.forward()
    second = []
    for off in range(1, N_EP):
        peer = other(ep, off, N_EP)
        second.append(push(rw_scr.at[peer], rw_ref.at[ep], s3.at[off], r3.at[off], "ep", peer))
    x_ref[ep] = x_scr[...]
    z_ref[ep] = z_scr[...]
    rw_ref[ep] = rw_scr[ep]
    ea_ring.last()
    x_ring.forward()
    z_ring.forward()
    x_ring.last()
    z_ring.last()
    for ring in (x_ring, z_ring, ea_ring):
        ring.finish()
    for copy in second:
        copy.wait()


def expert_kernel(
    x_ref, z_ref, rw_ref, ea_ref, w_up_ref, w_down_ref, part_ref, coeff_ref,
    rows_scr, z_scr, hid_scr, scaled_scr, cs_scr,
):
    e = pl.program_id(0)
    slots = lax.broadcasted_iota(jnp.int32, (CAP, TOK), 0).astype(F32)
    for j in range(N_EP):
        pick = (rw_ref[j, pl.ds(e, 1), :] == slots).astype(F32).astype(BF)
        rs = slice(j * CAP, j * CAP + CAP)
        rows_scr[rs, :] = dot(pick, x_ref[j]).astype(BF)
        z_scr[rs, :] = dot_nt(pick, z_ref[j]).astype(BF)
    for f in range(2):
        gate_cols = slice(f * 256, f * 256 + 256)
        up_cols = slice(FF + f * 256, FF + f * 256 + 256)
        pre_gate = dot(rows_scr[...], w_up_ref[0, :, gate_cols])
        pre_up = dot(rows_scr[...], w_up_ref[0, :, up_cols])
        for j in range(N_EP):
            rs = slice(j * CAP, j * CAP + CAP)
            gate = pre_gate[rs] + dot(z_scr[rs, 0:32], ea_ref[j, 0:32, gate_cols])
            up = pre_up[rs] + dot(z_scr[rs, 32:64], ea_ref[j, 32:64, gate_cols])
            hid_scr[rs, gate_cols] = (jax.nn.silu(gate) * up).astype(BF)
    for f in range(4):
        cols = slice(f * 256, f * 256 + 256)
        out = dot(hid_scr[...], w_down_ref[0, :, cols])
        for j in range(N_EP):
            rs = slice(j * CAP, j * CAP + CAP)
            hit = rw_ref[j, pl.ds(e, 1), :] == slots
            weight = jnp.sum(
                jnp.where(hit, rw_ref[j, pl.ds(e + 4, 1), :], 0.0), axis=1, keepdims=True
            )
            scaled_scr[j, e, :, cols] = (out[rs] * weight).astype(BF)
            if f == 0:
                coeff = dot_nt(hid_scr[rs, :], ea_ref[j, 64:96, :])
                cs_scr[j, e] = (coeff * weight).astype(BF)

    @pl.when(e == EXP_LOCAL - 1)
    def _():
        for j in range(N_EP):
            pick = jnp.concatenate(
                [(rw_ref[j, i : i + 1, :] == slots).astype(F32).astype(BF) for i in range(4)],
                axis=0,
            )
            part_ref[j] = dot_tn(pick, scaled_scr[j].reshape(4 * CAP, D)).astype(BF)
            coeff_ref[j] = dot_tn(cs_scr[j].reshape(4 * CAP, 32), pick).astype(BF)


def combine_kernel(
    lengths_ref, part_ref, coeff_ref, res_ref, rest_ref, out_ref,
    sib_in, sums, far_in, near_in, coeff_in, s1, r1, s2, r2,
):
    ep = lax.axis_index("ep")
    me = lax.axis_index("dp")
    barrier([("ep", N_EP)])
    up, down, far, sib = ring_ids(ep)
    half = TOK // 2
    low, high = pl.ds(0, half), pl.ds(half, half)
    c = lax.rem(ep, 2)
    order = [far, up, down, ep]
    pairs = []
    for i, dest in enumerate(order):
        pairs.append(
            push(part_ref.at[dest + 1 - 2 * c], sib_in.at[i], s1.at[i], r1.at[i], "ep", sib)
        )
    copies = []
    for off in range(1, N_EP):
        peer = other(ep, off, N_EP)
        copies.append(push(coeff_ref.at[peer], coeff_in.at[ep], s2.at[off], r2.at[off], "ep", peer))

    def pair_sum(i):
        pairs[i].wait_recv()
        return part_ref[order[i]].astype(F32) + sib_in[i].astype(F32)

    sums[0] = pair_sum(0).astype(BF)
    hop = [
        push(sums.at[0, low], far_in.at[0], s1.at[4], r1.at[4], "ep", up),
        push(sums.at[0, high], far_in.at[1], s1.at[5], r1.at[5], "ep", down),
    ]
    up_sum = pair_sum(1)
    sums[1, half:, :] = up_sum[half:].astype(BF)
    hop.append(push(sums.at[1, high], near_in.at[0, high], s1.at[6], r1.at[6], "ep", up))
    down_sum = pair_sum(2)
    sums[2, 0:half, :] = down_sum[0:half].astype(BF)
    hop.append(push(sums.at[2, low], near_in.at[1, low], s1.at[7], r1.at[7], "ep", down))
    hop[0].wait_recv()
    sums[1, 0:half, :] = (up_sum[0:half] + far_in[0].astype(F32)).astype(BF)
    hop.append(push(sums.at[1, low], near_in.at[0, low], s1.at[8], r1.at[8], "ep", up))
    hop[1].wait_recv()
    sums[2, half:, :] = (down_sum[half:] + far_in[1].astype(F32)).astype(BF)
    hop.append(push(sums.at[2, high], near_in.at[1, high], s1.at[9], r1.at[9], "ep", down))
    lane_first = first_request_lanes(lengths_ref, me * TOK)
    total = pair_sum(3)
    csum = coeff_ref[ep].astype(F32)
    for copy in copies:
        copy.wait()
    for off in range(1, N_EP):
        csum = csum + coeff_in[other(ep, off, N_EP)].astype(F32)
    for copy in hop[2:]:
        copy.wait_recv()
    total = total + near_in[0].astype(F32) + near_in[1].astype(F32)
    for copy in pairs + hop:
        copy.wait_send()
    lo_rows = jnp.where(lane_first, csum[0:16], 0.0).astype(BF)
    hi_rows = jnp.where(lane_first, 0.0, csum[16:32]).astype(BF)
    for block in range(8):
        delta = dot_tn(lo_rows, rest_ref[8 + block, 0:16, :]) + dot_tn(
            hi_rows, rest_ref[8 + block, 16:32, :]
        )
        cols = slice(block * 128, block * 128 + 128)
        out_ref[:, cols] = (res_ref[:, cols].astype(F32) + total[:, cols] + delta).astype(BF)


def vmem():
    return pl.BlockSpec(memory_space=pltpu.VMEM)


def smem():
    return pl.BlockSpec(memory_space=pltpu.SMEM)


def params(collective):
    return pltpu.CompilerParams(collective_id=collective, has_side_effects=True)


def shape(dims, dtype=BF):
    return jax.ShapeDtypeStruct(dims, dtype)


def per_device(
    tokens, lengths, adapter_ids, expert_ids, attn_gain, w_qkv, w_out, moe_gain,
    w_router, w_gate_up, w_down, adapter_in, adapter_out, adapter_expert,
):
    half = HEAD // 2
    frequency = THETA ** (-jnp.arange(half, dtype=F32) / half)
    dma = pltpu.SemaphoreType.DMA
    qkv_in, main, rest = pl.pallas_call(
        project_kernel,
        name="project",
        out_shape=(
            shape((N_DP, 192, TOK)),
            shape((N_DP, 96, 128)),
            shape((N_DP, 64, 128)),
        ),
        in_specs=[smem(), smem()] + [vmem()] * 7,
        out_specs=(vmem(),) * 3,
        scratch_shapes=[
            pltpu.VMEM((N_DP, 96, 128), BF),
            pltpu.VMEM((N_DP, 64, 128), BF),
            pltpu.VMEM((N_DP, 96, 128), BF),
            pltpu.VMEM((N_DP, 64, 128), BF),
            pltpu.VMEM((TOK, D), BF),
            pltpu.VMEM((TOK, QKV), F32),
            pltpu.VMEM((N_DP, 192, TOK), BF),
        ]
        + [dma((N_DP,))] * 12,
        compiler_params=params(0),
    )(
        lengths, adapter_ids, tokens, attn_gain, w_qkv, adapter_in, adapter_out,
        adapter_expert, frequency[:, None],
    )

    attended = pl.pallas_call(
        attention_kernel,
        name="attention",
        out_shape=shape((N_DP, HEAD, TOK)),
        in_specs=[smem(), vmem()],
        out_specs=vmem(),
        scratch_shapes=[pltpu.VMEM((N_DP * TOK, HEAD), BF)],
    )(lengths, qkv_in)

    residual, x_all, z_all, rw_all, ea_all = pl.pallas_call(
        route_kernel,
        name="route",
        out_shape=(
            shape((TOK, D)),
            shape((N_EP, TOK, D)),
            shape((N_EP, 64, TOK)),
            shape((N_EP, 8, TOK), F32),
            shape((N_EP, 96, FF)),
        ),
        in_specs=[smem()] + [vmem()] * 8,
        out_specs=(vmem(),) * 5,
        scratch_shapes=[
            pltpu.VMEM((N_DP, HEAD, TOK), BF),
            pltpu.VMEM((TOK, D), BF),
            pltpu.VMEM((64, TOK), BF),
            pltpu.VMEM((N_EP, 8, TOK), F32),
            pltpu.VMEM((96, FF), BF),
            dma((N_DP,)),
            dma((N_DP,)),
            dma((3, 9)),
            dma((3, 9)),
            dma((N_EP,)),
            dma((N_EP,)),
        ],
        compiler_params=params(1),
    )(
        lengths, attended, tokens, main, rest, w_out, moe_gain,
        jnp.transpose(w_router), jnp.transpose(expert_ids),
    )

    def whole(dims):
        return pl.BlockSpec(dims, lambda e: (0,) * len(dims))

    parts, coeffs = pl.pallas_call(
        expert_kernel,
        name="experts",
        grid=(EXP_LOCAL,),
        out_shape=(shape((N_EP, TOK, D)), shape((N_EP, 32, TOK))),
        in_specs=[
            whole((N_EP, TOK, D)),
            whole((N_EP, 64, TOK)),
            whole((N_EP, 8, TOK)),
            whole((N_EP, 96, FF)),
            pl.BlockSpec((1, D, 2 * FF), lambda e: (e, 0, 0)),
            pl.BlockSpec((1, FF, D), lambda e: (e, 0, 0)),
        ],
        out_specs=(whole((N_EP, TOK, D)), whole((N_EP, 32, TOK))),
        scratch_shapes=[
            pltpu.VMEM((N_EP * CAP, D), BF),
            pltpu.VMEM((N_EP * CAP, 64), BF),
            pltpu.VMEM((N_EP * CAP, FF), BF),
            pltpu.VMEM((N_EP, EXP_LOCAL, CAP, D), BF),
            pltpu.VMEM((N_EP, EXP_LOCAL, CAP, 32), BF),
        ],
    )(x_all, z_all, rw_all, ea_all, w_gate_up, w_down)

    return pl.pallas_call(
        combine_kernel,
        name="combine",
        out_shape=shape((TOK, D)),
        in_specs=[smem()] + [vmem()] * 4,
        out_specs=vmem(),
        scratch_shapes=[
            pltpu.VMEM((4, TOK, D), BF),
            pltpu.VMEM((3, TOK, D), BF),
            pltpu.VMEM((2, TOK // 2, D), BF),
            pltpu.VMEM((2, TOK, D), BF),
            pltpu.VMEM((N_EP, 32, TOK), BF),
            dma((10,)),
            dma((10,)),
            dma((N_EP,)),
            dma((N_EP,)),
        ],
        compiler_params=params(2),
    )(lengths, parts, coeffs, residual, rest)


def solution(mesh):
    return jax.shard_map(
        per_device,
        mesh=mesh,
        in_specs=(
            P(("ep", "dp"), None),
            P("ep", None),
            P(),
            P(("ep", "dp"), None),
            P(),
            P(),
            P(),
            P(),
            P(),
            P("ep", None, None),
            P("ep", None, None),
            P("dp", None, None),
            P("dp", None, None),
            P("dp", None, None),
        ),
        out_specs=P(("ep", "dp"), None),
        check_vma=False,
    )
```
